512 devices in a mesh: dp: 2 (over y_hi), gx: 32 (over x, z), gy: 8 (over y_lo, core).
Axes of the slice: x: 4, y: 8 (y_hi: 2, y_lo: 4; y = y_hi * 4 + y_lo), z: 8, core: 2. Of those that a mesh axis runs over, the one named last changes fastest.
Arguments:
- fields: bfloat16 [2, 16, 256, 32768], P('dp', None, 'gx', 'gy'), may hold values from -6 to 6
- pre_act: bfloat16 [2, 16, 256, 32768], P('dp', None, 'gx', 'gy'), may hold values from -6 to 6
- cotangent: bfloat16 [2, 16, 256, 32768], P('dp', None, 'gx', 'gy'), may hold values from -6 to 6
- spec_weight: bfloat16 [2, 32, 32, 16, 256], P(None, 'gx', None, 'gy'), may hold values from -12 to 12
- point_weight: bfloat16 [16, 16], replicated, may hold values from -1.5 to 1.5
Outputs:
- grad_fields: bfloat16 [2, 16, 256, 32768], P('dp', None, 'gx', 'gy')
- grad_spec: float32 [2, 32, 32, 16, 256], P(None, 'gx', None, 'gy')
The draws below stay inside these ranges and needn't reach their ends.
All inputs are finite; a program needn't handle non-finite values.
Results may differ from the reference program's by a relative error of at most 0.0098.
Values may be sent and summed in bfloat16 or wider, within the bound.
No kernel may reach another device: no remote copies, remote signals or barrier semaphores. Data moves between devices by JAX's collectives and lax.ppermute only.
A program may use at most 64 MiB of HBM per device.

```python
import math
import jax
import jax.numpy as jnp
from jax import lax

B = 2
C = 16
NX = 256
NY = 512
NZ = 64
MX = 32
MY = 32
MZ = 16
NYZ = 32768


def steps_of(own_key, extent, split, smallest, largest):
    def one(dim, parts):
        steps = jax.random.uniform(jax.random.fold_in(jax.random.fold_in(own_key, 6), dim), (parts,), jnp.float32, smallest / len(split), largest / len(split))
        return jnp.repeat(jnp.exp(steps), extent[dim] // parts).reshape((-1,) + (1,) * (len(extent) - dim - 1))

    loudness = one(*split[0])
    for cut in split[1:]:
        loudness = loudness * one(*cut)
    return loudness


def noise(own_key, dims, width, bound, pieces=(), kind=jnp.bfloat16):
    loudness = steps_of(own_key, dims, pieces, -0.22, 0.18) if pieces else 1.0
    drawn = jax.random.normal(own_key, dims, jnp.float32) * width * loudness
    return jnp.minimum(jnp.maximum(drawn, -bound), bound).astype(kind)


def setup_inputs(seed: int = 0) -> dict:
    key_of = jax.random.split(jax.random.key(seed), 6)
    fields = noise(key_of[0], (B, C, NX, NYZ), 1.0, 6.0, ((0, 2), (2, 32), (3, 8)))
    pre_act = noise(key_of[1], (B, C, NX, NYZ), 1.5, 6.0, ((0, 2), (2, 32), (3, 8)))
    cotangent = noise(key_of[2], (B, C, NX, NYZ), 1.0, 6.0, ((0, 2), (2, 32), (3, 8)))
    spec_weight = noise(key_of[3], (2, MX, MY, MZ, C * C), 3.0, 12.0, ((1, 32), (3, 8)))
    point_weight = noise(key_of[4], (C, C), C ** -0.5, 1.5)
    return {"fields": fields, "pre_act": pre_act, "cotangent": cotangent, "spec_weight": spec_weight, "point_weight": point_weight}


def kept_freqs(kept, length, both_signs):
    index = jnp.arange(kept, dtype=jnp.int32)
    if both_signs:
        return jnp.where(index < kept // 2, index, length - kept + index).astype(jnp.int32)
    return index

def phase(freqs, points, length):
    turns = points[:, None] * freqs[None, :] % length
    return turns.astype(jnp.float32) * (2.0 * math.pi / length)

def forward_table(kept, length):
    angle = phase(kept_freqs(kept, length, True), jnp.arange(length, dtype=jnp.int32), length)
    cosine = jnp.cos(angle)
    minus_sine = -jnp.sin(angle)
    upper = jnp.stack([cosine, minus_sine], axis=-1)
    lower = jnp.stack([-minus_sine, cosine], axis=-1)
    return jnp.stack([upper, lower], axis=1).astype(jnp.bfloat16)

def inverse_table(kept, length, positions):
    angle = phase(kept_freqs(kept, length, True), positions, length)
    cosine = jnp.transpose(jnp.cos(angle))
    sine = jnp.transpose(jnp.sin(angle))
    upper = jnp.stack([cosine, sine], axis=-1)
    lower = jnp.stack([-sine, cosine], axis=-1)
    return jnp.stack([upper, lower], axis=1).astype(jnp.bfloat16)

def z_forward_table():
    angle = phase(kept_freqs(MZ, NZ, False), jnp.arange(NZ, dtype=jnp.int32), NZ)
    return jnp.stack([jnp.cos(angle), -jnp.sin(angle)], axis=-1).reshape(NZ, 2 * MZ).astype(jnp.bfloat16)

def z_inverse_table():
    angle = jnp.transpose(phase(kept_freqs(MZ, NZ, False), jnp.arange(NZ, dtype=jnp.int32), NZ))
    return jnp.stack([jnp.cos(angle), -jnp.sin(angle)], axis=1).reshape(2 * MZ, NZ).astype(jnp.bfloat16)

def widen(table):
    return lax.optimization_barrier(table).astype(jnp.float32)

def gelu_slope(value):
    cdf = 0.5 * (1.0 + jax.scipy.special.erf(value * (1.0 / math.sqrt(2.0))))
    return cdf + value * jnp.exp(-0.5 * value * value) * (1.0 / math.sqrt(2.0 * math.pi))

def reference(fields, pre_act, cotangent, spec_weight, point_weight):
    highest = lax.Precision.HIGHEST
    grad_pre = (cotangent.astype(jnp.float32) * gelu_slope(pre_act.astype(jnp.float32))).astype(jnp.bfloat16)
    z_fwd = z_forward_table()
    x_fwd = widen(forward_table(MX, NX))
    y_fwd = widen(forward_table(MY, NY))
    y_back = widen(inverse_table(MY, NY, jnp.arange(NY, dtype=jnp.int32)))
    x_back = widen(inverse_table(MX, NX, jnp.arange(NX, dtype=jnp.int32)))
    z_back = z_inverse_table()
    stacked = jnp.concatenate([fields, grad_pre], axis=1).reshape(B * 2 * C, NX, NY, NZ)

    def forward_one(channel):
        z_spectra = jnp.dot(channel, z_fwd, preferred_element_type=jnp.float32).astype(jnp.bfloat16)
        z_spectra = z_spectra.reshape(NX, NY, MZ, 2).astype(jnp.float32)
        x_spectra = jnp.einsum('xyzr,xrkq->kyzq', z_spectra, x_fwd).astype(jnp.bfloat16)
        return jnp.einsum('kyzr,yrlq->klzq', x_spectra.astype(jnp.float32), y_fwd).astype(jnp.bfloat16)
    spectrum = lax.map(forward_one, stacked).reshape(B, 2, C, MX, MY, MZ, 2)
    field_hat = spectrum[:, 0].astype(jnp.float32)
    grad_hat_in = spectrum[:, 1].astype(jnp.float32)
    kz_index = jnp.arange(MZ, dtype=jnp.int32)
    weight_z = jnp.where(kz_index == 0, 1.0, 2.0).astype(jnp.float32) / float(NX * NY * NZ)
    scaled = grad_hat_in * weight_z[:, None]
    real_u, imag_u = (field_hat[..., 0], field_hat[..., 1])
    real_d, imag_d = (scaled[..., 0], scaled[..., 1])
    form = 'bixyz,boxyz->xyzio'
    real_w = jnp.einsum(form, real_u, real_d, precision=highest) + jnp.einsum(form, imag_u, imag_d, precision=highest)
    imag_w = jnp.einsum(form, real_u, imag_d, precision=highest) - jnp.einsum(form, imag_u, real_d, precision=highest)
    grad_spec = jnp.stack([real_w, imag_w], axis=0).reshape(2, MX, MY, MZ, C * C)
    weights = spec_weight.astype(jnp.float32).reshape(2, MX, MY, MZ, C, C)
    back_form = 'xyzio,boxyz->bixyz'
    real_g = jnp.einsum(back_form, weights[0], real_d, precision=highest) + jnp.einsum(back_form, weights[1], imag_d, precision=highest)
    imag_g = jnp.einsum(back_form, weights[0], imag_d, precision=highest) - jnp.einsum(back_form, weights[1], real_d, precision=highest)
    grad_hat = jnp.stack([real_g, imag_g], axis=-1).astype(jnp.bfloat16).reshape(B * C, MX, MY, MZ, 2)

    def inverse_one(channel):
        back_y = jnp.einsum('klzr,lryq->kyzq', channel.astype(jnp.float32), y_back).astype(jnp.bfloat16)
        back_x = jnp.einsum('kyzr,krxq->xyzq', back_y.astype(jnp.float32), x_back).astype(jnp.bfloat16)
        spectral = jnp.dot(back_x.reshape(NX, NY, 2 * MZ), z_back, preferred_element_type=jnp.float32)
        return spectral.reshape(NX, NY * NZ)
    spectral_part = lax.map(inverse_one, grad_hat).reshape(B, C, NX, NY * NZ)
    point_f = point_weight.astype(jnp.float32)
    outputs = []
    for sample in range(B):
        pointwise = jnp.einsum('io,oxq->ixq', point_f, grad_pre[sample].astype(jnp.float32))
        outputs.append((spectral_part[sample] + pointwise).astype(jnp.bfloat16))
    grad_fields = jnp.stack(outputs, axis=0)
    return (grad_fields, grad_spec)
```

```python
import math

import jax
import jax.numpy as jnp
import numpy as np
from jax import lax
from jax.experimental import pallas as pl
from jax.experimental.pallas import tpu as pltpu
from jax.sharding import PartitionSpec as P

C = 16
NX = 256
NY = 512
NZ = 64
MX = 32
MY = 32
MZ = 16
GROUP = 8

F32 = jnp.float32
BF16 = jnp.bfloat16
HIGHEST = lax.Precision.HIGHEST


def signed_freqs(kept, length):
    index = np.arange(kept)
    return np.where(index < kept // 2, index, length - kept + index)


def cos_sin(freqs, points, length):
    turns = points[:, None] * freqs[None, :] % length
    angle = turns.astype(np.float32) * np.float32(2.0 * math.pi / length)
    return np.cos(angle).astype(np.float32), np.sin(angle).astype(np.float32)


def z_block_table():
    cosine, sine = cos_sin(np.arange(MZ), np.arange(NZ), NZ)
    parts = np.stack([cosine.T, -sine.T], axis=1)
    same = np.eye(GROUP, dtype=np.float32)
    table = parts[:, :, None, None, :] * same[None, None, :, :, None]
    return table.reshape(2 * MZ * GROUP, GROUP * NZ).astype(BF16)


def y_block_tables(count, local_y, local_mz):
    cosine, sine = cos_sin(signed_freqs(MY, NY), np.arange(NY), NY)
    upper = np.stack([cosine, sine], axis=-1)
    lower = np.stack([-sine, cosine], axis=-1)
    table = np.stack([upper, lower], axis=0)
    table = table.reshape(2, count, local_y, MY, 2).transpose(1, 0, 3, 4, 2)
    same = np.eye(local_mz, dtype=np.float32)
    table = table[:, :, :, None, None, :, :] * same[None, None, None, :, :, None, None]
    return table.reshape(count, 2 * MY * local_mz, local_mz * 2 * local_y).astype(BF16)


def x_row_tables(count, local_x):
    cosine, sine = cos_sin(signed_freqs(MX, NX), np.arange(NX), NX)
    table = np.stack([cosine, sine], axis=0).reshape(2, count, local_x, MX)
    table = table.transpose(1, 0, 3, 2)
    return np.tile(table, (1, 1, 1, 128 // local_x)).astype(BF16)


def dot(left, right, dims, precision=None):
    return lax.dot_general(
        left, right, (dims, ((), ())), preferred_element_type=F32, precision=precision
    )


def gelu_slope(value):
    cdf = 0.5 * (1.0 + lax.erf(value * (1.0 / math.sqrt(2.0))))
    return cdf + value * jnp.exp(-0.5 * value * value) * (1.0 / math.sqrt(2.0 * math.pi))


def forward_zy(where, fields, pre_act, cotangent, z_table, y_table, grad_pre, pieces, lines):
    step = pl.program_id(0)
    slope = gelu_slope(pre_act[...].astype(F32))
    grad = (cotangent[...].astype(F32) * slope).astype(BF16)
    grad_pre[...] = grad
    both = jnp.concatenate([fields[...], grad], axis=0)
    spectra = dot(z_table[...], both, ((1,), (1,)))
    rows = pl.ds(pl.multiple_of(step * GROUP, GROUP), GROUP)
    lines[:, rows, :] = spectra.reshape(2 * MZ, GROUP, both.shape[0])

    @pl.when(step == pl.num_programs(0) - 1)
    def _():
        count = pieces.shape[0]
        per = 2 * MZ // count
        for index in range(count):
            block = lines[index * per : (index + 1) * per]
            block = block.reshape(per * block.shape[1], block.shape[2]).astype(BF16)
            pieces[index] = dot(y_table[0], block, ((1,), (0,))).astype(BF16)


def forward_x(where, arrived, x_rows, pieces):
    count = arrived.shape[0]
    total = arrived[0].astype(F32)
    for index in range(1, count):
        total = total + arrived[index].astype(F32)
    half = total.shape[0] // 2
    swapped = jnp.concatenate([total[half:], -total[:half]], axis=0).astype(BF16)
    total = total.astype(BF16)
    rows = 2 * C
    lanes = total.shape[1]
    local_x = lanes // rows
    owner = lax.broadcasted_iota(jnp.int32, (rows, lanes), 1) // local_x
    mask = owner == lax.broadcasted_iota(jnp.int32, (rows, lanes), 0)
    blocks = []
    for part in range(2):
        table = x_rows[0, part].astype(F32)
        table = jnp.concatenate([table] * (lanes // table.shape[1]), axis=1)
        table = jnp.where(mask[None], table[:, None, :], 0.0)
        blocks.append(table.reshape(MX * rows, lanes).astype(BF16))
    spectra = dot(blocks[0], total, ((1,), (1,))) + dot(blocks[1], swapped, ((1,), (1,)))
    pieces[...] = spectra.reshape(MX, rows, spectra.shape[1]).astype(BF16)


def mode_scale(where, rows, local_mz):
    line = lax.broadcasted_iota(jnp.int32, (rows, 1), 0) % local_mz + where[1] * local_mz
    return jnp.where(line == 0, 1.0, 2.0).astype(F32) / float(NX * NY * NZ)


def repeat_tables():
    lane = lax.broadcasted_iota(jnp.int32, (C, C * C), 1)
    row = lax.broadcasted_iota(jnp.int32, (C, C * C), 0)
    outer = (lane // C == row).astype(F32)
    inner = (lane % C == row).astype(F32)
    return outer, inner


def mode_products(where, arrived, weights, spectrum, grad_hat):
    count = arrived.shape[0]
    total = arrived[0].astype(F32)
    for index in range(1, count):
        total = total + arrived[index].astype(F32)
    total = total.astype(BF16)
    spectrum[...] = total
    modes = total.shape[1] // 2
    outer, inner = repeat_tables()
    grads = dot(total[C:], inner.astype(BF16), ((0,), (0,)))
    scale = mode_scale(where, modes, modes // MY)
    real_d = grads[:modes] * scale
    imag_d = grads[modes:] * scale
    real_w = weights[0].astype(F32)
    imag_w = weights[1].astype(F32)
    products = jnp.concatenate(
        [real_w * real_d + imag_w * imag_d, real_w * imag_d - imag_w * real_d], axis=0
    )
    values = dot(outer, products, ((1,), (1,)), HIGHEST).astype(BF16)
    grad_hat[...] = jnp.broadcast_to(values[None], grad_hat.shape)


def weight_grads(where, own, other, result):
    modes = own.shape[1] // 2
    outer, inner = repeat_tables()
    outer = outer.astype(BF16)
    inner = inner.astype(BF16)
    scale = mode_scale(where, modes, modes // MY)
    real_sum = jnp.zeros((modes, C * C), F32)
    imag_sum = jnp.zeros((modes, C * C), F32)
    for spectrum in (own, other):
        values = spectrum[...]
        field = dot(values[:C], outer, ((0,), (0,)))
        grads = dot(values[C:], inner, ((0,), (0,)))
        real_u, imag_u = field[:modes], field[modes:]
        real_d, imag_d = grads[:modes] * scale, grads[modes:] * scale
        real_sum = real_sum + (real_u * real_d + imag_u * imag_d)
        imag_sum = imag_sum + (real_u * imag_d - imag_u * real_d)
    result[0] = real_sum
    result[1] = imag_sum


def inverse_x(where, arrived, x_rows, result):
    lanes = x_rows.shape[3]
    local_x = lanes // C
    owner = lax.broadcasted_iota(jnp.int32, (C, lanes), 1) // local_x
    mask = owner == lax.broadcasted_iota(jnp.int32, (C, lanes), 0)
    values = arrived[...].reshape(MX * C, arrived.shape[2])
    half = values.shape[1] // 2
    swapped = jnp.concatenate([-values[:, half:], values[:, :half]], axis=1)
    sums = None
    for part, operand in enumerate((values, swapped)):
        table = jnp.where(mask[None], x_rows[0, part].astype(F32)[:, None, :], 0.0)
        table = table.reshape(MX * C, lanes).astype(BF16)
        term = dot(operand, table, ((0,), (0,)))
        sums = term if sums is None else sums + term
    result[...] = jnp.broadcast_to(sums.astype(BF16)[None], result.shape)


def inverse_yz(where, arrived, grad_pre, z_table, y_table, point, result, lines, mixing):
    step = pl.program_id(0)
    rows = mixing.shape[0]
    local_x = rows // C

    @pl.when(step == 0)
    def _():
        count = arrived.shape[0]
        per = 2 * MZ // count
        for index in range(count):
            block = dot(y_table[0], arrived[index], ((0,), (0,)))
            lines[index * per : (index + 1) * per] = block.reshape(per, -1, rows)
        row = lax.broadcasted_iota(jnp.int32, (rows, C), 0) // local_x
        pick = (row == lax.broadcasted_iota(jnp.int32, (rows, C), 1)).astype(BF16)
        spread = dot(pick, point[...], ((1,), (0,))).astype(BF16)
        spread = dot(spread, pick, ((1,), (1,)))
        left = lax.broadcasted_iota(jnp.int32, (rows, rows), 0) % local_x
        right = lax.broadcasted_iota(jnp.int32, (rows, rows), 1) % local_x
        mixing[...] = jnp.where(left == right, spread, 0.0).astype(BF16)

    window = pl.ds(pl.multiple_of(step * GROUP, GROUP), GROUP)
    block = lines[:, window, :].reshape(2 * MZ * GROUP, rows).astype(BF16)
    spectral = dot(block, z_table[...], ((0,), (0,)))
    result[...] = (spectral + dot(mixing[...], grad_pre[...], ((1,), (0,)))).astype(BF16)


def whole(shape):
    return pl.BlockSpec(shape, lambda *_: (0,) * len(shape))


def at_gx(shape):
    return pl.BlockSpec((1,) + shape[1:], lambda i, w: (w[0],) + (0,) * (len(shape) - 1))


def at_gy(shape):
    return pl.BlockSpec((1,) + shape[1:], lambda i, w: (w[1],) + (0,) * (len(shape) - 1))


def call(body, name, grid, in_specs, out_specs, out_shape, scratch=()):
    return pl.pallas_call(
        body,
        name=name,
        grid_spec=pltpu.PrefetchScalarGridSpec(
            num_scalar_prefetch=1,
            grid=(grid,),
            in_specs=in_specs,
            out_specs=out_specs,
            scratch_shapes=scratch,
        ),
        out_shape=out_shape,
        compiler_params=pltpu.CompilerParams(
            dimension_semantics=("arbitrary",), vmem_limit_bytes=16 << 20
        ),
    )


def on_device(fields, pre_act, cotangent, spec_weight, point_weight):
    count_x = lax.axis_size("gx")
    count_y = lax.axis_size("gy")
    _, channels, local_x, local_yz = fields.shape
    local_y = local_yz // NZ
    local_mz = spec_weight.shape[3]
    rows = channels * local_x
    modes = MY * local_mz
    groups = local_y // GROUP
    width = GROUP * NZ
    where = jnp.stack([lax.axis_index("gx"), lax.axis_index("gy")]).astype(jnp.int32)
    z_table = jnp.asarray(z_block_table())
    y_table = jnp.asarray(y_block_tables(count_y, local_y, local_mz))
    x_rows = jnp.asarray(x_row_tables(count_x, local_x))
    shape = jax.ShapeDtypeStruct
    columns = pl.BlockSpec((rows, width), lambda i, w: (0, i))

    grad_pre, pieces = call(
        forward_zy,
        "forward_zy",
        groups,
        [columns, columns, columns, whole(z_table.shape), at_gy(y_table.shape)],
        (columns, whole((count_y, 2 * modes, 2 * rows))),
        (shape((rows, local_yz), BF16), shape((count_y, 2 * modes, 2 * rows), BF16)),
        [pltpu.VMEM((2 * MZ, local_y, 2 * rows), F32)],
    )(
        where,
        fields.reshape(rows, local_yz),
        pre_act.reshape(rows, local_yz),
        cotangent.reshape(rows, local_yz),
        z_table,
        y_table,
    )
    arrived = lax.all_to_all(pieces, "gy", split_axis=0, concat_axis=0, tiled=True)
    pieces = call(
        forward_x,
        "forward_x",
        1,
        [whole(arrived.shape), at_gx(x_rows.shape)],
        whole((MX, 2 * C, 2 * modes)),
        shape((MX, 2 * C, 2 * modes), BF16),
    )(where, arrived, x_rows)
    arrived = lax.all_to_all(pieces, "gx", split_axis=0, concat_axis=0, tiled=True)
    spectrum, grad_hat = call(
        mode_products,
        "mode_products",
        1,
        [whole(arrived.shape), whole((2, modes, C * C))],
        (whole((2 * C, 2 * modes)), whole((count_x, C, 2 * modes))),
        (shape((2 * C, 2 * modes), BF16), shape((count_x, C, 2 * modes), BF16)),
    )(where, arrived, spec_weight.reshape(2, modes, C * C))
    other = lax.ppermute(spectrum, "dp", [(0, 1), (1, 0)])
    gathered = lax.all_to_all(grad_hat, "gx", split_axis=0, concat_axis=0, tiled=True)
    back_x = call(
        inverse_x,
        "inverse_x",
        1,
        [whole(gathered.shape), at_gx(x_rows.shape)],
        whole((count_y, 2 * modes, rows)),
        shape((count_y, 2 * modes, rows), BF16),
    )(where, gathered, x_rows)
    gathered = lax.all_to_all(back_x, "gy", split_axis=0, concat_axis=0, tiled=True)
    grad_spec = call(
        weight_grads,
        "weight_grads",
        1,
        [whole(spectrum.shape), whole(other.shape)],
        whole((2, modes, C * C)),
        shape((2, modes, C * C), F32),
    )(where, spectrum, other)
    grad_fields = call(
        inverse_yz,
        "inverse_yz",
        groups,
        [
            whole(gathered.shape),
            columns,
            whole(z_table.shape),
            at_gy(y_table.shape),
            whole(point_weight.shape),
        ],
        columns,
        shape((rows, local_yz), BF16),
        [pltpu.VMEM((2 * MZ, local_y, rows), F32), pltpu.VMEM((rows, rows), BF16)],
    )(where, gathered, grad_pre, z_table, y_table, point_weight)
    return grad_fields.reshape(fields.shape), grad_spec.reshape(spec_weight.shape)


def solution(mesh):
    placed = (
        P("dp", None, "gx", "gy"),
        P("dp", None, "gx", "gy"),
        P("dp", None, "gx", "gy"),
        P(None, "gx", None, "gy", None),
        P(),
    )
    return jax.shard_map(
        on_device,
        mesh=mesh,
        in_specs=placed,
        out_specs=(P("dp", None, "gx", "gy"), P(None, "gx", None, "gy", None)),
        check_vma=False,
    )
```

```python
import math

import jax
import jax.numpy as jnp
import numpy as np
from jax import lax
from jax.experimental import pallas as pl
from jax.experimental.pallas import tpu as pltpu
from jax.sharding import PartitionSpec as P

C = 16
NX = 256
NY = 512
NZ = 64
MX = 32
MY = 32
MZ = 16
GROUP = 8

F32 = jnp.float32
BF16 = jnp.bfloat16
HIGHEST = lax.Precision.HIGHEST


def signed_freqs(kept, length):
    index = np.arange(kept)
    return np.where(index < kept // 2, index, length - kept + index)


def cos_sin(freqs, points, length):
    turns = points[:, None] * freqs[None, :] % length
    angle = turns.astype(np.float32) * np.float32(2.0 * math.pi / length)
    return np.cos(angle).astype(np.float32), np.sin(angle).astype(np.float32)


def z_block_table():
    cosine, sine = cos_sin(np.arange(MZ), np.arange(NZ), NZ)
    parts = np.stack([cosine.T, -sine.T], axis=1)
    same = np.eye(GROUP, dtype=np.float32)
    table = parts[:, :, None, None, :] * same[None, None, :, :, None]
    return table.reshape(2 * MZ * GROUP, GROUP * NZ).astype(BF16)


def y_block_tables(count, local_y, local_mz):
    cosine, sine = cos_sin(signed_freqs(MY, NY), np.arange(NY), NY)
    upper = np.stack([cosine, sine], axis=-1)
    lower = np.stack([-sine, cosine], axis=-1)
    table = np.stack([upper, lower], axis=0)
    table = table.reshape(2, count, local_y, MY, 2).transpose(1, 0, 3, 4, 2)
    same = np.eye(local_mz, dtype=np.float32)
    table = table[:, :, :, None, None, :, :] * same[None, None, None, :, :, None, None]
    return table.reshape(count, 2 * MY * local_mz, local_mz * 2 * local_y).astype(BF16)


def x_row_tables(count, local_x):
    cosine, sine = cos_sin(signed_freqs(MX, NX), np.arange(NX), NX)
    table = np.stack([cosine, sine], axis=0).reshape(2, count, local_x, MX)
    table = table.transpose(1, 0, 3, 2)
    return np.tile(table, (1, 1, 1, 128 // local_x)).astype(BF16)


def dot(left, right, dims, precision=None):
    return lax.dot_general(
        left, right, (dims, ((), ())), preferred_element_type=F32, precision=precision
    )


def gelu_slope(value):
    cdf = 0.5 * (1.0 + lax.erf(value * (1.0 / math.sqrt(2.0))))
    return cdf + value * jnp.exp(-0.5 * value * value) * (1.0 / math.sqrt(2.0 * math.pi))


def transform_group(block, z_table, y_table, store, count, lines):
    step = pl.program_id(0)
    for index in range(block.shape[1] // z_table.shape[1]):
        width = z_table.shape[1]
        part = block[:, index * width : (index + 1) * width]
        spectra = dot(z_table[...], part, ((1,), (1,)))
        start = pl.multiple_of(step * (block.shape[1] // NZ), GROUP) + index * GROUP
        lines[:, pl.ds(start, GROUP), :] = spectra.reshape(2 * MZ, GROUP, block.shape[0])

    @pl.when(step == pl.num_programs(0) - 1)
    def _():
        per = 2 * MZ // count
        for index in range(count):
            chunk = lines[index * per : (index + 1) * per]
            chunk = chunk.reshape(per * chunk.shape[1], chunk.shape[2]).astype(BF16)
            store(index, dot(y_table[0], chunk, ((1,), (0,))).astype(BF16))


def forward_grads(where, pre_act, cotangent, z_table, y_table, grad_pre, pieces, lines):
    slope = gelu_slope(pre_act[...].astype(F32))
    grad = (cotangent[...].astype(F32) * slope).astype(BF16)
    grad_pre[...] = grad

    def store(index, value):
        pieces[index] = value

    transform_group(grad, z_table, y_table, store, pieces.shape[0], lines)


def forward_fields(where, fields, z_table, y_table, kept, given, lines):
    side = where[1] % 2

    def store(index, value):
        @pl.when(side == index % 2)
        def _():
            kept[index // 2] = value

        @pl.when(side != index % 2)
        def _():
            given[index // 2] = value

    transform_group(fields[...], z_table, y_table, store, 2 * kept.shape[0], lines)


def add_halves(where, kept, taken, *sums):
    chip = where[1] // 2
    for distance, total in enumerate(sums):
        index = lax.rem(chip + distance, len(sums))
        total[...] = (kept[index].astype(F32) + taken[index].astype(F32)).astype(BF16)


def forward_fields_x(where, *refs):
    lines, x_rows, pieces = refs[:-2], refs[-2], refs[-1]
    total = lines[0][...].astype(F32)
    for term in lines[1:]:
        total = total + term[...].astype(F32)
    transform_x(total, x_rows, pieces)


def forward_x(where, arrived, x_rows, pieces):
    transform_x(add_up(arrived), x_rows, pieces)


def transform_x(total, x_rows, pieces):
    half = total.shape[0] // 2
    swapped = jnp.concatenate([total[half:], -total[:half]], axis=0).astype(BF16)
    total = total.astype(BF16)
    rows = C
    lanes = total.shape[1]
    local_x = lanes // rows
    owner = lax.broadcasted_iota(jnp.int32, (rows, lanes), 1) // local_x
    mask = owner == lax.broadcasted_iota(jnp.int32, (rows, lanes), 0)
    blocks = []
    for part in range(2):
        table = jnp.where(mask[None], x_rows[0, part].astype(F32)[:, None, :], 0.0)
        blocks.append(table.reshape(MX * rows, lanes).astype(BF16))
    spectra = dot(blocks[0], total, ((1,), (1,))) + dot(blocks[1], swapped, ((1,), (1,)))
    pieces[...] = spectra.reshape(MX, rows, spectra.shape[1]).astype(BF16)


def mode_scale(where, rows, local_mz):
    line = lax.broadcasted_iota(jnp.int32, (rows, 1), 0) % local_mz + where[1] * local_mz
    return jnp.where(line == 0, 1.0, 2.0).astype(F32) / float(NX * NY * NZ)


def repeat_tables():
    lane = lax.broadcasted_iota(jnp.int32, (C, C * C), 1)
    row = lax.broadcasted_iota(jnp.int32, (C, C * C), 0)
    outer = (lane // C == row).astype(F32)
    inner = (lane % C == row).astype(F32)
    return outer, inner


def add_up(arrived, rows=slice(None)):
    total = arrived[0, rows].astype(F32)
    for index in range(1, arrived.shape[0]):
        total = total + arrived[index, rows].astype(F32)
    return total


def mode_products(where, arrived, weights, fields, spectrum, pieces):
    total = add_up(arrived).astype(BF16)
    spectrum[...] = total
    modes = total.shape[1] // 2
    outer, inner = repeat_tables()
    grads = dot(total, inner.astype(BF16), ((0,), (0,)))
    scale = mode_scale(where, modes, modes // MY)
    real_d = grads[:modes] * scale
    imag_d = grads[modes:] * scale
    real_w = weights[0].astype(F32)
    imag_w = weights[1].astype(F32)
    products = jnp.concatenate(
        [real_w * real_d + imag_w * imag_d, real_w * imag_d - imag_w * real_d], axis=0
    )
    values = dot(outer, products, ((1,), (1,)), HIGHEST).astype(BF16)
    pieces[:, :C] = jnp.broadcast_to(values[None], fields.shape)
    pieces[:, C:] = fields[...]


def join_spectra(where, arrived, grads, spectra):
    spectra[:C] = add_up(arrived, slice(C, None)).astype(BF16)
    spectra[C:] = grads[...]


def weight_grads(where, own, other, result):
    modes = own.shape[1] // 2
    outer, inner = repeat_tables()
    outer = outer.astype(BF16)
    inner = inner.astype(BF16)
    scale = mode_scale(where, modes, modes // MY)
    real_sum = jnp.zeros((modes, C * C), F32)
    imag_sum = jnp.zeros((modes, C * C), F32)
    for spectra in (own, other):
        values = spectra[...]
        field = dot(values[:C], outer, ((0,), (0,)))
        grads = dot(values[C:], inner, ((0,), (0,)))
        real_u, imag_u = field[:modes], field[modes:]
        real_d, imag_d = grads[:modes] * scale, grads[modes:] * scale
        real_sum = real_sum + (real_u * real_d + imag_u * imag_d)
        imag_sum = imag_sum + (real_u * imag_d - imag_u * real_d)
    result[0] = real_sum
    result[1] = imag_sum


def inverse_x(where, arrived, x_rows, result):
    lanes = x_rows.shape[3]
    local_x = lanes // C
    owner = lax.broadcasted_iota(jnp.int32, (C, lanes), 1) // local_x
    mask = owner == lax.broadcasted_iota(jnp.int32, (C, lanes), 0)
    values = arrived[:, :C].reshape(MX * C, arrived.shape[2])
    half = values.shape[1] // 2
    swapped = jnp.concatenate([-values[:, half:], values[:, :half]], axis=1)
    sums = None
    for part, operand in enumerate((values, swapped)):
        table = jnp.where(mask[None], x_rows[0, part].astype(F32)[:, None, :], 0.0)
        table = table.reshape(MX * C, lanes).astype(BF16)
        term = dot(operand, table, ((0,), (0,)))
        sums = term if sums is None else sums + term
    result[...] = jnp.broadcast_to(sums.astype(BF16)[None], result.shape)


def inverse_yz(where, arrived, grad_pre, z_table, y_table, point, result, lines, mixing):
    step = pl.program_id(0)
    rows = mixing.shape[0]
    local_x = rows // C

    @pl.when(step == 0)
    def _():
        count = arrived.shape[0]
        per = 2 * MZ // count
        for index in range(count):
            block = dot(y_table[0], arrived[index], ((0,), (0,)))
            lines[index * per : (index + 1) * per] = block.reshape(per, -1, rows)
        row = lax.broadcasted_iota(jnp.int32, (rows, C), 0) // local_x
        pick = (row == lax.broadcasted_iota(jnp.int32, (rows, C), 1)).astype(BF16)
        spread = dot(pick, point[...], ((1,), (0,))).astype(BF16)
        spread = dot(spread, pick, ((1,), (1,)))
        left = lax.broadcasted_iota(jnp.int32, (rows, rows), 0) % local_x
        right = lax.broadcasted_iota(jnp.int32, (rows, rows), 1) % local_x
        mixing[...] = jnp.where(left == right, spread, 0.0).astype(BF16)

    width = z_table.shape[1]
    for index in range(result.shape[1] // width):
        start = pl.multiple_of(step * (result.shape[1] // NZ), GROUP) + index * GROUP
        block = lines[:, pl.ds(start, GROUP), :].reshape(2 * MZ * GROUP, rows).astype(BF16)
        spectral = dot(block, z_table[...], ((0,), (0,)))
        part = slice(index * width, (index + 1) * width)
        mixed = dot(mixing[...], grad_pre[:, part], ((1,), (0,)))
        result[:, part] = (spectral + mixed).astype(BF16)


def whole(shape):
    return pl.BlockSpec(shape, lambda *_: (0,) * len(shape))


def at_gx(shape):
    return pl.BlockSpec((1,) + shape[1:], lambda i, w: (w[0],) + (0,) * (len(shape) - 1))


def at_gy(shape):
    return pl.BlockSpec((1,) + shape[1:], lambda i, w: (w[1],) + (0,) * (len(shape) - 1))


def call(body, grid, in_specs, out_specs, out_shape, scratch=(), vmem=16):
    return pl.pallas_call(
        body,
        grid_spec=pltpu.PrefetchScalarGridSpec(
            num_scalar_prefetch=1,
            grid=(grid,),
            in_specs=in_specs,
            out_specs=out_specs,
            scratch_shapes=scratch,
        ),
        out_shape=out_shape,
        compiler_params=pltpu.CompilerParams(
            dimension_semantics=("arbitrary",), vmem_limit_bytes=vmem << 20
        ),
    )


def exchange(pieces, axis):
    return lax.all_to_all(pieces, axis, split_axis=0, concat_axis=0, tiled=True)


def on_device(fields, pre_act, cotangent, spec_weight, point_weight):
    count_x = lax.axis_size("gx")
    count_y = lax.axis_size("gy")
    _, channels, local_x, local_yz = fields.shape
    local_y = local_yz // NZ
    local_mz = spec_weight.shape[3]
    rows = channels * local_x
    modes = MY * local_mz
    steps = 4
    where = jnp.stack([lax.axis_index("gx"), lax.axis_index("gy")]).astype(jnp.int32)
    z_table = jnp.asarray(z_block_table())
    y_table = jnp.asarray(y_block_tables(count_y, local_y, local_mz))
    x_rows = jnp.asarray(x_row_tables(count_x, local_x))
    shape = jax.ShapeDtypeStruct
    columns = pl.BlockSpec((rows, local_yz // steps), lambda i, w: (0, i))
    y_pieces = (count_y, 2 * modes, rows)
    x_pieces = (count_x, C, 2 * modes)
    lines = pltpu.VMEM((2 * MZ, local_y, rows), F32)
    tables = [whole(z_table.shape), at_gy(y_table.shape)]

    grad_pre, grad_lines = call(
        forward_grads,
        steps,
        [columns, columns] + tables,
        (columns, whole(y_pieces)),
        (shape((rows, local_yz), BF16), shape(y_pieces, BF16)),
        [lines],
        vmem=60,
    )(
        where,
        pre_act.reshape(rows, local_yz),
        cotangent.reshape(rows, local_yz),
        z_table,
        y_table,
    )
    grad_lines = exchange(grad_lines, "gy")
    half = (count_y // 2,) + y_pieces[1:]
    line = y_pieces[1:]
    kept, given = call(
        forward_fields,
        steps,
        [columns] + tables,
        (whole(half), whole(half)),
        (shape(half, BF16), shape(half, BF16)),
        [lines],
        vmem=60,
    )(where, fields.reshape(rows, local_yz), z_table, y_table)
    taken = lax.ppermute(given, "gy", [(i, i ^ 1) for i in range(count_y)])
    field_lines = call(
        add_halves,
        1,
        [whole(half), whole(half)],
        (whole(line),) * half[0],
        (shape(line, BF16),) * half[0],
    )(where, kept, taken)
    field_lines = [field_lines[0]] + [
        lax.ppermute(
            field_lines[k], "gy", [(i, (i + 2 * k) % count_y) for i in range(count_y)]
        )
        for k in range(1, half[0])
    ]
    field_modes = call(
        forward_fields_x,
        1,
        [whole(line)] * half[0] + [at_gx(x_rows.shape)],
        whole(x_pieces),
        shape(x_pieces, BF16),
    )(where, *field_lines, x_rows)
    grad_modes = call(
        forward_x, 1, [whole(y_pieces), at_gx(x_rows.shape)], whole(x_pieces), shape(x_pieces, BF16)
    )(where, grad_lines, x_rows)
    grad_modes = exchange(grad_modes, "gx")
    both = (count_x, 2 * C, 2 * modes)
    grad_spectrum, pieces = call(
        mode_products,
        1,
        [whole(x_pieces), whole((2, modes, C * C)), whole(x_pieces)],
        (whole((C, 2 * modes)), whole(both)),
        (shape((C, 2 * modes), BF16), shape(both, BF16)),
    )(where, grad_modes, spec_weight.reshape(2, modes, C * C), field_modes)
    arrived = exchange(pieces, "gx")
    back_x = call(
        inverse_x, 1, [whole(both), at_gx(x_rows.shape)], whole(y_pieces), shape(y_pieces, BF16)
    )(where, arrived, x_rows)
    gathered = exchange(back_x, "gy")
    spectra = call(
        join_spectra,
        1,
        [whole(both), whole((C, 2 * modes))],
        whole((2 * C, 2 * modes)),
        shape((2 * C, 2 * modes), BF16),
    )(where, arrived, grad_spectrum)
    other = lax.ppermute(spectra, "dp", [(0, 1), (1, 0)])
    grad_spec = call(
        weight_grads,
        1,
        [whole(spectra.shape), whole(spectra.shape)],
        whole((2, modes, C * C)),
        shape((2, modes, C * C), F32),
    )(where, spectra, other)
    grad_fields = call(
        inverse_yz,
        steps,
        [whole(y_pieces), columns] + tables + [whole(point_weight.shape)],
        columns,
        shape((rows, local_yz), BF16),
        [lines, pltpu.VMEM((rows, rows), BF16)],
    )(where, gathered, grad_pre, z_table, y_table, point_weight)
    return grad_fields.reshape(fields.shape), grad_spec.reshape(spec_weight.shape)


def solution(mesh):
    placed = (
        P("dp", None, "gx", "gy"),
        P("dp", None, "gx", "gy"),
        P("dp", None, "gx", "gy"),
        P(None, "gx", None, "gy", None),
        P(),
    )

    return jax.shard_map(
        on_device,
        mesh=mesh,
        in_specs=placed,
        out_specs=(P("dp", None, "gx", "gy"), P(None, "gx", None, "gy", None)),
        check_vma=False,
    )
```

```python
import math

import jax
import jax.numpy as jnp
import numpy as np
from jax import lax
from jax.experimental import pallas as pl
from jax.experimental.pallas import tpu as pltpu
from jax.sharding import PartitionSpec as P

C = 16
NX = 256
NY = 512
NZ = 64
MX = 32
MY = 32
MZ = 16
GROUP = 8

F32 = jnp.float32
BF16 = jnp.bfloat16
HIGHEST = lax.Precision.HIGHEST


def signed_freqs(kept, length):
    index = np.arange(kept)
    return np.where(index < kept // 2, index, length - kept + index)


def cos_sin(freqs, points, length):
    turns = points[:, None] * freqs[None, :] % length
    angle = turns.astype(np.float32) * np.float32(2.0 * math.pi / length)
    return np.cos(angle).astype(np.float32), np.sin(angle).astype(np.float32)


def z_block_table():
    cosine, sine = cos_sin(np.arange(MZ), np.arange(NZ), NZ)
    parts = np.stack([cosine.T, -sine.T], axis=1)
    same = np.eye(GROUP, dtype=np.float32)
    table = parts[:, :, None, None, :] * same[None, None, :, :, None]
    return table.reshape(2 * MZ * GROUP, GROUP * NZ).astype(BF16)


def y_block_tables(count, local_y, local_mz):
    cosine, sine = cos_sin(signed_freqs(MY, NY), np.arange(NY), NY)
    upper = np.stack([cosine, sine], axis=-1)
    lower = np.stack([-sine, cosine], axis=-1)
    table = np.stack([upper, lower], axis=0)
    table = table.reshape(2, count, local_y, MY, 2).transpose(1, 0, 3, 4, 2)
    same = np.eye(local_mz, dtype=np.float32)
    table = table[:, :, :, None, None, :, :] * same[None, None, None, :, :, None, None]
    return table.reshape(count, 2 * MY * local_mz, local_mz * 2 * local_y).astype(BF16)


def x_row_tables(count, local_x):
    cosine, sine = cos_sin(signed_freqs(MX, NX), np.arange(NX), NX)
    table = np.stack([cosine, sine], axis=0).reshape(2, count, local_x, MX)
    table = table.transpose(1, 0, 3, 2)
    return np.tile(table, (1, 1, 1, 128 // local_x)).astype(BF16)


def dot(left, right, dims, precision=None):
    return lax.dot_general(
        left, right, (dims, ((), ())), preferred_element_type=F32, precision=precision
    )


def gelu_slope(value):
    cdf = 0.5 * (1.0 + lax.erf(value * (1.0 / math.sqrt(2.0))))
    return cdf + value * jnp.exp(-0.5 * value * value) * (1.0 / math.sqrt(2.0 * math.pi))


def copies_in(sources, targets, sems, groups):
    width = targets[0].shape[1] // groups
    copies = []
    for group in range(groups):
        lanes = pl.ds(group * width, width)
        copies.append(
            [
                pltpu.make_async_copy(
                    source.at[:, lanes], target.at[:, lanes], sems.at[index, group]
                )
                for index, (source, target) in enumerate(zip(sources, targets))
            ]
        )
    return copies


def forward_zy(
    fields, pre_act, cotangent, z_source, y_source, grad_pre, pieces,
    fields_in, pre_in, cotangent_in, z_table, y_table, lines, sems, table_sems,
):
    groups = sems.shape[1]
    tables = [
        pltpu.make_async_copy(z_source, z_table, table_sems.at[0]),
        pltpu.make_async_copy(y_source.at[lax.axis_index("gy")], y_table, table_sems.at[1]),
    ]
    copies = copies_in(
        (pre_act, cotangent, fields), (pre_in, cotangent_in, fields_in), sems, groups
    )
    for copy in copies[0] + tables[:1]:
        copy.start()
    for group in copies[1:]:
        for copy in group:
            copy.start()
    tables[1].start()
    width = pre_in.shape[1] // groups
    pair = []
    for group, arrived in enumerate(copies):
        for copy in arrived:
            copy.wait()
        part = slice(group * width, (group + 1) * width)
        slope = gelu_slope(pre_in[:, part].astype(F32))
        grad = (cotangent_in[:, part].astype(F32) * slope).astype(BF16)
        grad_pre[:, part] = grad
        both = jnp.concatenate([fields_in[:, part], grad], axis=0)
        if group == 0:
            tables[0].wait()
        spectra = dot(z_table[...], both, ((1,), (1,)))
        pair.append(spectra.reshape(2 * MZ, GROUP, both.shape[0]))
        if len(pair) == 2:
            rows = slice((group - 1) * GROUP, (group + 1) * GROUP)
            lines[:, rows, :] = jnp.concatenate(pair, axis=1).astype(BF16)
            pair = []
    tables[1].wait()
    count = pieces.shape[0]
    per = 2 * MZ // count
    for index in range(count):
        block = lines[index * per : (index + 1) * per]
        block = block.reshape(per * block.shape[1], block.shape[2])
        pieces[index] = dot(y_table[...], block, ((1,), (0,))).astype(BF16)


def add_up(arrived):
    total = arrived[0].astype(F32)
    for index in range(1, arrived.shape[0]):
        total = total + arrived[index].astype(F32)
    return total


def x_blocks(x_rows):
    lanes = x_rows.shape[3]
    owner = lax.broadcasted_iota(jnp.int32, (C, lanes), 1) // (lanes // C)
    mask = owner == lax.broadcasted_iota(jnp.int32, (C, lanes), 0)
    rows = x_rows[lax.axis_index("gx")].astype(F32)
    blocks = []
    for part in range(2):
        table = jnp.where(mask[None], rows[part][:, None, :], 0.0)
        blocks.append(table.reshape(MX * C, lanes).astype(BF16))
    return blocks


def forward_x(arrived, x_rows, pieces):
    blocks = x_blocks(x_rows)
    total = add_up(arrived)
    half = total.shape[0] // 2
    swapped = jnp.concatenate([total[half:], -total[:half]], axis=0).astype(BF16)
    total = total.astype(BF16)
    lanes = blocks[0].shape[1]
    for part in range(2):
        own = slice(part * lanes, (part + 1) * lanes)
        spectra = dot(blocks[0], total[:, own], ((1,), (1,)))
        spectra = spectra + dot(blocks[1], swapped[:, own], ((1,), (1,)))
        spectra = spectra.reshape(MX, C, spectra.shape[1]).astype(BF16)
        pieces[:, part * C : (part + 1) * C, :] = spectra


def mode_scale(rows, local_mz):
    line = lax.broadcasted_iota(jnp.int32, (rows, 1), 0) % local_mz
    line = line + lax.axis_index("gy") * local_mz
    return jnp.where(line == 0, 1.0, 2.0).astype(F32) / float(NX * NY * NZ)


def repeat_tables():
    lane = lax.broadcasted_iota(jnp.int32, (C, C * C), 1)
    row = lax.broadcasted_iota(jnp.int32, (C, C * C), 0)
    outer = (lane // C == row).astype(F32)
    inner = (lane % C == row).astype(F32)
    return outer, inner


def mode_products(arrived, weights, spectrum, grad_hat):
    total = add_up(arrived).astype(BF16)
    spectrum[...] = total
    modes = total.shape[1] // 2
    outer, inner = repeat_tables()
    grads = dot(total[C:], inner.astype(BF16), ((0,), (0,)))
    scale = mode_scale(modes, modes // MY)
    real_d = grads[:modes] * scale
    imag_d = grads[modes:] * scale
    real_w = weights[0, 0].astype(F32).reshape(modes, C * C)
    imag_w = weights[1, 0].astype(F32).reshape(modes, C * C)
    products = jnp.concatenate(
        [real_w * real_d + imag_w * imag_d, real_w * imag_d - imag_w * real_d], axis=0
    )
    values = dot(outer, products, ((1,), (1,)), HIGHEST).astype(BF16)
    grad_hat[...] = jnp.broadcast_to(values[None], grad_hat.shape)


def weight_grads(own, other, result):
    modes = own.shape[1] // 2
    outer, inner = repeat_tables()
    outer = outer.astype(BF16)
    inner = inner.astype(BF16)
    scale = mode_scale(modes, modes // MY)
    real_sum = jnp.zeros((modes, C * C), F32)
    imag_sum = jnp.zeros((modes, C * C), F32)
    for spectrum in (own, other):
        values = spectrum[...]
        field = dot(values[:C], outer, ((0,), (0,)))
        grads = dot(values[C:], inner, ((0,), (0,)))
        real_u, imag_u = field[:modes], field[modes:]
        real_d, imag_d = grads[:modes] * scale, grads[modes:] * scale
        real_sum = real_sum + (real_u * real_d + imag_u * imag_d)
        imag_sum = imag_sum + (real_u * imag_d - imag_u * real_d)
    for part, total in enumerate((real_sum, imag_sum)):
        result[part, 0] = total.reshape(result.shape[2:])


def inverse_x(arrived, x_rows, result):
    blocks = x_blocks(x_rows)
    values = arrived[...].reshape(MX * C, arrived.shape[2])
    half = values.shape[1] // 2
    swapped = jnp.concatenate([-values[:, half:], values[:, :half]], axis=1)
    sums = dot(values, blocks[0], ((0,), (0,))) + dot(swapped, blocks[1], ((0,), (0,)))
    result[...] = jnp.broadcast_to(sums.astype(BF16)[None], result.shape)


def inverse_yz(
    arrived, grad_pre, z_table, y_tables, point, result, lines, staged, sems
):
    y_table = y_tables[lax.axis_index("gy")]
    rows = staged.shape[0]
    local_x = rows // C
    row = lax.broadcasted_iota(jnp.int32, (rows, C), 0) // local_x
    pick = (row == lax.broadcasted_iota(jnp.int32, (rows, C), 1)).astype(BF16)
    spread = dot(pick, point[...], ((1,), (0,))).astype(BF16)
    spread = dot(spread, pick, ((1,), (1,)))
    left = lax.broadcasted_iota(jnp.int32, (rows, rows), 0) % local_x
    right = lax.broadcasted_iota(jnp.int32, (rows, rows), 1) % local_x
    mixing = jnp.where(left == right, spread, 0.0).astype(BF16)
    count = arrived.shape[0]
    per = 2 * MZ // count
    for index in range(count):
        block = dot(y_table, arrived[index], ((0,), (0,)))
        lines[index * per : (index + 1) * per] = block.reshape(per, -1, rows)
    width = z_table.shape[1]
    copies = []
    for group in range(result.shape[1] // width):
        block = lines[:, group * GROUP : (group + 1) * GROUP, :]
        block = block.reshape(2 * MZ * GROUP, rows).astype(BF16)
        spectral = dot(block, z_table[...], ((0,), (0,)))
        part = slice(group * width, (group + 1) * width)
        mixed = dot(mixing, grad_pre[:, part], ((1,), (0,)))
        staged[:, part] = (spectral + mixed).astype(BF16)
        copy = pltpu.make_async_copy(
            staged.at[:, pl.ds(group * width, width)],
            result.at[:, pl.ds(group * width, width)],
            sems.at[group],
        )
        copy.start()
        copies.append(copy)
    for copy in copies:
        copy.wait()


VMEM = pl.BlockSpec(memory_space=pltpu.VMEM)
HBM = pl.BlockSpec(memory_space=pltpu.HBM)


def call(body, ins, outs, scratch=(), vmem=24):
    values = [
        pltpu.with_memory_space_constraint(value, spec.memory_space) for value, spec in ins
    ]
    specs = [spec for _, spec in ins]
    shapes = [
        pltpu.VMEM(shape, dtype) if spec is VMEM else jax.ShapeDtypeStruct(shape, dtype)
        for shape, dtype, spec in outs
    ]
    return pl.pallas_call(
        body,
        in_specs=specs,
        out_specs=[spec for _, _, spec in outs],
        out_shape=shapes,
        scratch_shapes=list(scratch),
        compiler_params=pltpu.CompilerParams(vmem_limit_bytes=vmem << 20),
    )(*values)


def exchange(pieces, axis):
    return lax.all_to_all(pieces, axis, split_axis=0, concat_axis=0, tiled=True)


def on_device(fields, pre_act, cotangent, spec_weight, point_weight):
    count_x = lax.axis_size("gx")
    count_y = lax.axis_size("gy")
    _, channels, local_x, local_yz = fields.shape
    local_y = local_yz // NZ
    local_mz = spec_weight.shape[3]
    rows = channels * local_x
    modes = MY * local_mz
    groups = local_y // GROUP
    z_table = jnp.asarray(z_block_table())
    y_table = jnp.asarray(y_block_tables(count_y, local_y, local_mz))
    x_rows = jnp.asarray(x_row_tables(count_x, local_x))
    whole = (rows, local_yz)
    dma = pltpu.SemaphoreType.DMA

    grad_pre, pieces = call(
        forward_zy,
        [
            (fields.reshape(whole), HBM),
            (pre_act.reshape(whole), HBM),
            (cotangent.reshape(whole), HBM),
            (z_table, HBM),
            (y_table, HBM),
        ],
        [(whole, BF16, VMEM), ((count_y, 2 * modes, 2 * rows), BF16, VMEM)],
        [pltpu.VMEM(whole, BF16)] * 3
        + [
            pltpu.VMEM(z_table.shape, BF16),
            pltpu.VMEM(y_table.shape[1:], BF16),
            pltpu.VMEM((2 * MZ, local_y, 2 * rows), BF16),
            dma((3, groups)),
            dma((2,)),
        ],
    )
    arrived = exchange(pieces, "gy")
    (pieces,) = call(
        forward_x,
        [(arrived, VMEM), (x_rows, VMEM)],
        [((count_x, 2 * C, 2 * modes), BF16, VMEM)],
    )
    arrived = exchange(pieces, "gx")
    spectrum, pieces = call(
        mode_products,
        [(arrived, VMEM), (spec_weight, VMEM)],
        [((2 * C, 2 * modes), BF16, VMEM), ((count_x, C, 2 * modes), BF16, VMEM)],
    )
    arrived = exchange(pieces, "gx")
    other = lax.ppermute(spectrum, "dp", [(0, 1), (1, 0)])
    (grad_spec,) = call(
        weight_grads,
        [(spectrum, VMEM), (other, VMEM)],
        [(spec_weight.shape, F32, pl.BlockSpec())],
    )
    (pieces,) = call(
        inverse_x,
        [(arrived, VMEM), (x_rows, VMEM)],
        [((count_y, 2 * modes, rows), BF16, VMEM)],
    )
    arrived = exchange(pieces, "gy")
    (grad_fields,) = call(
        inverse_yz,
        [
            (arrived, VMEM),
            (grad_pre, VMEM),
            (z_table, VMEM),
            (y_table, VMEM),
            (point_weight, VMEM),
        ],
        [(whole, BF16, HBM)],
        [
            pltpu.VMEM((2 * MZ, local_y, rows), F32),
            pltpu.VMEM(whole, BF16),
            dma((groups,)),
        ],
    )
    return grad_fields.reshape(fields.shape), grad_spec


def solution(mesh):
    placed = (
        P("dp", None, "gx", "gy"),
        P("dp", None, "gx", "gy"),
        P("dp", None, "gx", "gy"),
        P(None, "gx", None, "gy", None),
        P(),
    )

    return jax.shard_map(
        on_device,
        mesh=mesh,
        in_specs=placed,
        out_specs=(P("dp", None, "gx", "gy"), P(None, "gx", None, "gy", None)),
        check_vma=False,
    )
```

```python
import math

import jax
import jax.numpy as jnp
import numpy as np
from jax import lax
from jax.experimental import pallas as pl
from jax.experimental.pallas import tpu as pltpu
from jax.sharding import PartitionSpec as P

C = 16
NX = 256
NY = 512
NZ = 64
MX = 32
MY = 32
MZ = 16
GROUP = 8

F32 = jnp.float32
BF16 = jnp.bfloat16
HIGHEST = lax.Precision.HIGHEST


def signed_freqs(kept, length):
    index = np.arange(kept)
    return np.where(index < kept // 2, index, length - kept + index)


def cos_sin(freqs, points, length):
    turns = points[:, None] * freqs[None, :] % length
    angle = turns.astype(np.float32) * np.float32(2.0 * math.pi / length)
    return np.cos(angle).astype(np.float32), np.sin(angle).astype(np.float32)


def z_block_table():
    cosine, sine = cos_sin(np.arange(MZ), np.arange(NZ), NZ)
    parts = np.stack([cosine.T, -sine.T], axis=1)
    same = np.eye(GROUP, dtype=np.float32)
    table = parts[:, :, None, None, :] * same[None, None, :, :, None]
    return table.reshape(2 * MZ * GROUP, GROUP * NZ).astype(BF16)


def y_block_tables(count, local_y, local_mz):
    cosine, sine = cos_sin(signed_freqs(MY, NY), np.arange(NY), NY)
    upper = np.stack([cosine, sine], axis=-1)
    lower = np.stack([-sine, cosine], axis=-1)
    table = np.stack([upper, lower], axis=0)
    table = table.reshape(2, count, local_y, MY, 2).transpose(1, 0, 3, 4, 2)
    same = np.eye(local_mz, dtype=np.float32)
    table = table[:, :, :, None, None, :, :] * same[None, None, None, :, :, None, None]
    return table.reshape(count, 2 * MY * local_mz, local_mz * 2 * local_y).astype(BF16)


def x_row_tables(count, local_x):
    cosine, sine = cos_sin(signed_freqs(MX, NX), np.arange(NX), NX)
    table = np.stack([cosine, sine], axis=0).reshape(2, count, local_x, MX)
    table = table.transpose(1, 0, 3, 2)
    return np.tile(table, (1, 1, 1, 128 // local_x)).astype(BF16)


def dot(left, right, dims, precision=None):
    return lax.dot_general(
        left, right, (dims, ((), ())), preferred_element_type=F32, precision=precision
    )


def gelu_slope(value):
    cdf = 0.5 * (1.0 + lax.erf(value * (1.0 / math.sqrt(2.0))))
    return cdf + value * jnp.exp(-0.5 * value * value) * (1.0 / math.sqrt(2.0 * math.pi))


def copies_in(sources, targets, sems):
    width = targets[0].shape[1] // sems.shape[1]
    copies = []
    for chunk in range(sems.shape[1]):
        lanes = pl.ds(chunk * width, width)
        copies.append(
            [
                pltpu.make_async_copy(
                    source.at[:, lanes], target.at[:, lanes], sems.at[index, chunk]
                )
                for index, (source, target) in enumerate(zip(sources, targets))
            ]
        )
    return copies


def forward_zy(
    fields, pre_act, cotangent, z_source, y_source, grad_pre, kept, given,
    fields_in, pre_in, cotangent_in, z_table, y_table, lines, sems, table_sems,
):
    groups = pre_act.shape[1] // z_source.shape[1]
    per_chunk = groups // sems.shape[1]
    tables = [
        pltpu.make_async_copy(z_source, z_table, table_sems.at[0]),
        pltpu.make_async_copy(y_source.at[lax.axis_index("gy")], y_table, table_sems.at[1]),
    ]
    copies = copies_in(
        (pre_act, cotangent, fields), (pre_in, cotangent_in, fields_in), sems
    )
    for copy in copies[0] + tables[:1]:
        copy.start()
    for chunk in copies[1:]:
        for copy in chunk:
            copy.start()
    tables[1].start()
    width = pre_in.shape[1] // groups
    pair = []
    for group in range(groups):
        if group % per_chunk == 0:
            for copy in copies[group // per_chunk]:
                copy.wait()
        part = slice(group * width, (group + 1) * width)
        slope = gelu_slope(pre_in[:, part].astype(F32))
        grad = (cotangent_in[:, part].astype(F32) * slope).astype(BF16)
        grad_pre[:, part] = grad
        both = jnp.concatenate([fields_in[:, part], grad], axis=0)
        if group == 0:
            tables[0].wait()
        spectra = dot(z_table[...], both, ((1,), (1,)))
        pair.append(spectra.reshape(2 * MZ, GROUP, both.shape[0]))
        if len(pair) == 2:
            rows = slice((group - 1) * GROUP, (group + 1) * GROUP)
            lines[:, rows, :] = jnp.concatenate(pair, axis=1).astype(BF16)
            pair = []
    tables[1].wait()
    side = lax.axis_index("gy") % 2
    count = 2 * kept.shape[0]
    per = 2 * MZ // count
    for index in range(count // 2):
        for pieces, offset in ((given, 1 - side), (kept, side)):
            first = (2 * index + offset) * per
            block = lines[pl.ds(first, per)]
            block = block.reshape(per * block.shape[1], block.shape[2])
            pieces[index] = dot(y_table[...], block, ((1,), (0,))).astype(BF16)


def add_halves(kept, taken, *sums):
    chip = lax.axis_index("gy") // 2
    for distance, total in enumerate(sums):
        index = lax.rem(chip + distance, len(sums))
        total[...] = (kept[index].astype(F32) + taken[index].astype(F32)).astype(BF16)


def add_up(arrived):
    total = arrived[0].astype(F32)
    for index in range(1, arrived.shape[0]):
        total = total + arrived[index].astype(F32)
    return total


def x_blocks(x_rows):
    lanes = x_rows.shape[3]
    owner = lax.broadcasted_iota(jnp.int32, (C, lanes), 1) // (lanes // C)
    mask = owner == lax.broadcasted_iota(jnp.int32, (C, lanes), 0)
    rows = x_rows[lax.axis_index("gx")].astype(F32)
    blocks = []
    for part in range(2):
        table = jnp.where(mask[None], rows[part][:, None, :], 0.0)
        blocks.append(table.reshape(MX * C, lanes).astype(BF16))
    return blocks


def forward_x(*refs):
    lines, x_rows, pieces = refs[:-2], refs[-2], refs[-1]
    blocks = x_blocks(x_rows)
    total = lines[0][...].astype(F32)
    for term in lines[1:]:
        total = total + term[...].astype(F32)
    half = total.shape[0] // 2
    swapped = jnp.concatenate([total[half:], -total[:half]], axis=0).astype(BF16)
    total = total.astype(BF16)
    lanes = blocks[0].shape[1]
    for part in range(2):
        own = slice(part * lanes, (part + 1) * lanes)
        spectra = dot(blocks[0], total[:, own], ((1,), (1,)))
        spectra = spectra + dot(blocks[1], swapped[:, own], ((1,), (1,)))
        spectra = spectra.reshape(MX, C, spectra.shape[1]).astype(BF16)
        pieces[:, part * C : (part + 1) * C, :] = spectra


def mode_scale(rows, local_mz):
    line = lax.broadcasted_iota(jnp.int32, (rows, 1), 0) % local_mz
    line = line + lax.axis_index("gy") * local_mz
    return jnp.where(line == 0, 1.0, 2.0).astype(F32) / float(NX * NY * NZ)


def repeat_tables():
    lane = lax.broadcasted_iota(jnp.int32, (C, C * C), 1)
    row = lax.broadcasted_iota(jnp.int32, (C, C * C), 0)
    outer = (lane // C == row).astype(F32)
    inner = (lane % C == row).astype(F32)
    return outer, inner


def mode_products(arrived, weights, spectrum, grad_hat):
    total = add_up(arrived).astype(BF16)
    spectrum[...] = total
    modes = total.shape[1] // 2
    outer, inner = repeat_tables()
    grads = dot(total[C:], inner.astype(BF16), ((0,), (0,)))
    scale = mode_scale(modes, modes // MY)
    real_d = grads[:modes] * scale
    imag_d = grads[modes:] * scale
    real_w = weights[0, 0].astype(F32).reshape(modes, C * C)
    imag_w = weights[1, 0].astype(F32).reshape(modes, C * C)
    products = jnp.concatenate(
        [real_w * real_d + imag_w * imag_d, real_w * imag_d - imag_w * real_d], axis=0
    )
    values = dot(outer, products, ((1,), (1,)), HIGHEST).astype(BF16)
    grad_hat[...] = jnp.broadcast_to(values[None], grad_hat.shape)


def weight_grads(own, other, result):
    modes = own.shape[1] // 2
    outer, inner = repeat_tables()
    outer = outer.astype(BF16)
    inner = inner.astype(BF16)
    scale = mode_scale(modes, modes // MY)
    real_sum = jnp.zeros((modes, C * C), F32)
    imag_sum = jnp.zeros((modes, C * C), F32)
    for spectrum in (own, other):
        values = spectrum[...]
        field = dot(values[:C], outer, ((0,), (0,)))
        grads = dot(values[C:], inner, ((0,), (0,)))
        real_u, imag_u = field[:modes], field[modes:]
        real_d, imag_d = grads[:modes] * scale, grads[modes:] * scale
        real_sum = real_sum + (real_u * real_d + imag_u * imag_d)
        imag_sum = imag_sum + (real_u * imag_d - imag_u * real_d)
    for part, total in enumerate((real_sum, imag_sum)):
        result[part, 0] = total.reshape(result.shape[2:])


def inverse_x(arrived, x_rows, result):
    blocks = x_blocks(x_rows)
    values = arrived[...].reshape(MX * C, arrived.shape[2])
    half = values.shape[1] // 2
    swapped = jnp.concatenate([-values[:, half:], values[:, :half]], axis=1)
    sums = dot(values, blocks[0], ((0,), (0,))) + dot(swapped, blocks[1], ((0,), (0,)))
    result[...] = jnp.broadcast_to(sums.astype(BF16)[None], result.shape)


def inverse_yz(
    arrived, grad_pre, z_table, y_tables, point, result, lines, staged, sems
):
    y_table = y_tables[lax.axis_index("gy")]
    rows = staged.shape[0]
    local_x = rows // C
    row = lax.broadcasted_iota(jnp.int32, (rows, C), 0) // local_x
    pick = (row == lax.broadcasted_iota(jnp.int32, (rows, C), 1)).astype(BF16)
    spread = dot(pick, point[...], ((1,), (0,))).astype(BF16)
    spread = dot(spread, pick, ((1,), (1,)))
    left = lax.broadcasted_iota(jnp.int32, (rows, rows), 0) % local_x
    right = lax.broadcasted_iota(jnp.int32, (rows, rows), 1) % local_x
    mixing = jnp.where(left == right, spread, 0.0).astype(BF16)
    count = arrived.shape[0]
    per = 2 * MZ // count
    for index in range(count):
        block = dot(y_table, arrived[index], ((0,), (0,)))
        lines[index * per : (index + 1) * per] = block.reshape(per, -1, rows)
    width = z_table.shape[1]
    copies = []
    for group in range(result.shape[1] // width):
        block = lines[:, group * GROUP : (group + 1) * GROUP, :]
        block = block.reshape(2 * MZ * GROUP, rows).astype(BF16)
        spectral = dot(block, z_table[...], ((0,), (0,)))
        part = slice(group * width, (group + 1) * width)
        mixed = dot(mixing, grad_pre[:, part], ((1,), (0,)))
        staged[:, part] = (spectral + mixed).astype(BF16)
        copy = pltpu.make_async_copy(
            staged.at[:, pl.ds(group * width, width)],
            result.at[:, pl.ds(group * width, width)],
            sems.at[group],
        )
        copy.start()
        copies.append(copy)
    for copy in copies:
        copy.wait()


VMEM = pl.BlockSpec(memory_space=pltpu.VMEM)
HBM = pl.BlockSpec(memory_space=pltpu.HBM)


def call(body, ins, outs, scratch=(), vmem=24):
    values = [
        pltpu.with_memory_space_constraint(value, spec.memory_space) for value, spec in ins
    ]
    specs = [spec for _, spec in ins]
    shapes = [
        pltpu.VMEM(shape, dtype) if spec is VMEM else jax.ShapeDtypeStruct(shape, dtype)
        for shape, dtype, spec in outs
    ]
    return pl.pallas_call(
        body,
        in_specs=specs,
        out_specs=[spec for _, _, spec in outs],
        out_shape=shapes,
        scratch_shapes=list(scratch),
        compiler_params=pltpu.CompilerParams(vmem_limit_bytes=vmem << 20),
    )(*values)


def run_forward_zy(fields, pre_act, cotangent, z_table, y_table, local_mz):
    rows, local_yz = fields.shape
    local_y = local_yz // NZ
    modes = MY * local_mz
    half = (MZ // local_mz // 2, 2 * modes, 2 * rows)
    whole = (rows, local_yz)
    dma = pltpu.SemaphoreType.DMA
    return call(
        forward_zy,
        [(fields, HBM), (pre_act, HBM), (cotangent, HBM), (z_table, HBM), (y_table, HBM)],
        [(whole, BF16, VMEM), (half, BF16, VMEM), (half, BF16, VMEM)],
        [pltpu.VMEM(whole, BF16)] * 3
        + [
            pltpu.VMEM(z_table.shape, BF16),
            pltpu.VMEM(y_table.shape[1:], BF16),
            pltpu.VMEM((2 * MZ, local_y, 2 * rows), BF16),
            dma((3, 2)),
            dma((2,)),
        ],
    )


def run_inverse_yz(arrived, grad_pre, z_table, y_table, point_weight):
    rows, local_yz = grad_pre.shape
    local_y = local_yz // NZ
    groups = local_y // GROUP
    (grad_fields,) = call(
        inverse_yz,
        [
            (arrived, VMEM),
            (grad_pre, VMEM),
            (z_table, VMEM),
            (y_table, VMEM),
            (point_weight, VMEM),
        ],
        [((rows, local_yz), BF16, HBM)],
        [
            pltpu.VMEM((2 * MZ, local_y, rows), F32),
            pltpu.VMEM((rows, local_yz), BF16),
            pltpu.SemaphoreType.DMA((groups,)),
        ],
    )
    return grad_fields


def exchange(pieces, axis):
    return lax.all_to_all(pieces, axis, split_axis=0, concat_axis=0, tiled=True)


def on_device(fields, pre_act, cotangent, spec_weight, point_weight):
    count_x = lax.axis_size("gx")
    count_y = lax.axis_size("gy")
    _, channels, local_x, local_yz = fields.shape
    local_y = local_yz // NZ
    local_mz = spec_weight.shape[3]
    rows = channels * local_x
    modes = MY * local_mz
    z_table = jnp.asarray(z_block_table())
    y_table = jnp.asarray(y_block_tables(count_y, local_y, local_mz))
    x_rows = jnp.asarray(x_row_tables(count_x, local_x))
    whole = (rows, local_yz)

    grad_pre, kept, given = run_forward_zy(
        fields.reshape(whole),
        pre_act.reshape(whole),
        cotangent.reshape(whole),
        z_table,
        y_table,
        local_mz,
    )
    taken = lax.ppermute(given, "gy", [(i, i ^ 1) for i in range(count_y)])
    chips = count_y // 2
    lines = call(
        add_halves,
        [(kept, VMEM), (taken, VMEM)],
        [((2 * modes, 2 * rows), BF16, VMEM)] * chips,
    )
    lines = [lines[0]] + [
        lax.ppermute(lines[k], "gy", [(i, (i + 2 * k) % count_y) for i in range(count_y)])
        for k in range(1, chips)
    ]
    (pieces,) = call(
        forward_x,
        [(line, VMEM) for line in lines] + [(x_rows, VMEM)],
        [((count_x, 2 * C, 2 * modes), BF16, VMEM)],
    )
    arrived = exchange(pieces, "gx")
    spectrum, pieces = call(
        mode_products,
        [(arrived, VMEM), (spec_weight, VMEM)],
        [((2 * C, 2 * modes), BF16, VMEM), ((count_x, C, 2 * modes), BF16, VMEM)],
    )
    arrived = exchange(pieces, "gx")
    other = lax.ppermute(spectrum, "dp", [(0, 1), (1, 0)])
    (grad_spec,) = call(
        weight_grads,
        [(spectrum, VMEM), (other, VMEM)],
        [(spec_weight.shape, F32, pl.BlockSpec())],
    )
    (pieces,) = call(
        inverse_x,
        [(arrived, VMEM), (x_rows, VMEM)],
        [((count_y, 2 * modes, rows), BF16, VMEM)],
    )
    arrived = exchange(pieces, "gy")
    grad_fields = run_inverse_yz(arrived, grad_pre, z_table, y_table, point_weight)
    return grad_fields.reshape(fields.shape), grad_spec


def solution(mesh):
    placed = (
        P("dp", None, "gx", "gy"),
        P("dp", None, "gx", "gy"),
        P("dp", None, "gx", "gy"),
        P(None, "gx", None, "gy", None),
        P(),
    )

    return jax.shard_map(
        on_device,
        mesh=mesh,
        in_specs=placed,
        out_specs=(P("dp", None, "gx", "gy"), P(None, "gx", None, "gy", None)),
        check_vma=False,
    )
```

```python
import functools
import math

import jax
import jax.numpy as jnp
import numpy as np
from jax import lax
from jax.experimental import pallas as pl
from jax.experimental.pallas import tpu as pltpu
from jax.sharding import PartitionSpec as P

C = 16
NX = 256
NY = 512
NZ = 64
MX = 32
MY = 32
MZ = 16
GROUP = 8

F32 = jnp.float32
BF16 = jnp.bfloat16
HIGHEST = lax.Precision.HIGHEST


def signed_freqs(kept, length):
    index = np.arange(kept)
    return np.where(index < kept // 2, index, length - kept + index)


def cos_sin(freqs, points, length):
    turns = points[:, None] * freqs[None, :] % length
    angle = turns.astype(np.float32) * np.float32(2.0 * math.pi / length)
    return np.cos(angle).astype(np.float32), np.sin(angle).astype(np.float32)


def z_block_table():
    cosine, sine = cos_sin(np.arange(MZ), np.arange(NZ), NZ)
    parts = np.stack([cosine.T, -sine.T], axis=1)
    same = np.eye(GROUP, dtype=np.float32)
    table = parts[:, :, None, None, :] * same[None, None, :, :, None]
    return table.reshape(2 * MZ * GROUP, GROUP * NZ).astype(BF16)


def y_block_tables(count, local_y, local_mz):
    cosine, sine = cos_sin(signed_freqs(MY, NY), np.arange(NY), NY)
    upper = np.stack([cosine, sine], axis=-1)
    lower = np.stack([-sine, cosine], axis=-1)
    table = np.stack([upper, lower], axis=0)
    table = table.reshape(2, count, local_y, MY, 2).transpose(1, 0, 3, 4, 2)
    same = np.eye(local_mz, dtype=np.float32)
    table = table[:, :, :, None, None, :, :] * same[None, None, None, :, :, None, None]
    return table.reshape(count, 2 * MY * local_mz, local_mz * 2 * local_y).astype(BF16)


def x_row_tables(count, local_x):
    cosine, sine = cos_sin(signed_freqs(MX, NX), np.arange(NX), NX)
    table = np.stack([cosine, sine], axis=0).reshape(2, count, local_x, MX)
    table = table.transpose(1, 0, 3, 2)
    return np.tile(table, (1, 1, 1, 128 // local_x)).astype(BF16)


def dot(left, right, dims, precision=None):
    return lax.dot_general(
        left, right, (dims, ((), ())), preferred_element_type=F32, precision=precision
    )


def gelu_slope(value):
    cdf = 0.5 * (1.0 + lax.erf(value * (1.0 / math.sqrt(2.0))))
    return cdf + value * jnp.exp(-0.5 * value * value) * (1.0 / math.sqrt(2.0 * math.pi))


def copies_in(sources, targets, sems):
    width = targets[0].shape[1] // sems.shape[1]
    copies = []
    for chunk in range(sems.shape[1]):
        lanes = pl.ds(chunk * width, width)
        copies.append(
            [
                pltpu.make_async_copy(
                    source.at[:, lanes], target.at[:, lanes], sems.at[index, chunk]
                )
                for index, (source, target) in enumerate(zip(sources, targets))
            ]
        )
    return copies


def forward_zy(
    fields, pre_act, cotangent, z_source, y_source, grad_pre, kept, given,
    fields_in, pre_in, cotangent_in, z_table, y_table, lines, sems, table_sems,
):
    groups = pre_act.shape[1] // z_source.shape[1]
    per_chunk = groups // sems.shape[1]
    tables = [
        pltpu.make_async_copy(z_source, z_table, table_sems.at[0]),
        pltpu.make_async_copy(y_source.at[lax.axis_index("gy")], y_table, table_sems.at[1]),
    ]
    copies = copies_in(
        (pre_act, cotangent, fields), (pre_in, cotangent_in, fields_in), sems
    )
    for copy in copies[0] + tables[:1]:
        copy.start()
    for chunk in copies[1:]:
        for copy in chunk:
            copy.start()
    tables[1].start()
    width = pre_in.shape[1] // groups
    pair = []
    for group in range(groups):
        if group % per_chunk == 0:
            for copy in copies[group // per_chunk]:
                copy.wait()
        part = slice(group * width, (group + 1) * width)
        slope = gelu_slope(pre_in[:, part].astype(F32))
        grad = (cotangent_in[:, part].astype(F32) * slope).astype(BF16)
        grad_pre[:, part] = grad
        both = jnp.concatenate([fields_in[:, part], grad], axis=0)
        if group == 0:
            tables[0].wait()
        spectra = dot(z_table[...], both, ((1,), (1,)))
        pair.append(spectra.reshape(2 * MZ, GROUP, both.shape[0]))
        if len(pair) == 2:
            rows = slice((group - 1) * GROUP, (group + 1) * GROUP)
            lines[:, rows, :] = jnp.concatenate(pair, axis=1).astype(BF16)
            pair = []
    tables[1].wait()
    side = lax.axis_index("gy") % 2
    count = 2 * kept.shape[0]
    per = 2 * MZ // count
    for index in range(count // 2):
        for pieces, offset in ((given, 1 - side), (kept, side)):
            first = (2 * index + offset) * per
            block = lines[pl.ds(first, per)]
            block = block.reshape(per * block.shape[1], block.shape[2])
            pieces[index] = dot(y_table[...], block, ((1,), (0,))).astype(BF16)


def add_halves(bit, kept, taken, keep, give):
    side = lax.axis_index("gy") // bit % 2
    for index in range(keep.shape[0]):
        for total, offset in ((give, 1 - side), (keep, side)):
            place = 2 * index + offset
            total[index] = (kept[place].astype(F32) + taken[place].astype(F32)).astype(BF16)


def join_halves(bit, own, taken, joined):
    side = lax.axis_index("gy") // bit % 2
    for index in range(own.shape[0]):
        joined[2 * index + side] = own[index]
        joined[2 * index + 1 - side] = taken[index]


def add_up(arrived):
    total = arrived[0].astype(F32)
    for index in range(1, arrived.shape[0]):
        total = total + arrived[index].astype(F32)
    return total


def x_blocks(x_rows):
    lanes = x_rows.shape[3]
    owner = lax.broadcasted_iota(jnp.int32, (C, lanes), 1) // (lanes // C)
    mask = owner == lax.broadcasted_iota(jnp.int32, (C, lanes), 0)
    rows = x_rows[lax.axis_index("gx")].astype(F32)
    blocks = []
    for part in range(2):
        table = jnp.where(mask[None], rows[part][:, None, :], 0.0)
        blocks.append(table.reshape(MX * C, lanes).astype(BF16))
    return blocks


def forward_x(kept, taken, x_rows, pieces):
    blocks = x_blocks(x_rows)
    total = kept[0].astype(F32) + taken[0].astype(F32)
    half = total.shape[0] // 2
    swapped = jnp.concatenate([total[half:], -total[:half]], axis=0).astype(BF16)
    total = total.astype(BF16)
    lanes = blocks[0].shape[1]
    for part in range(2):
        own = slice(part * lanes, (part + 1) * lanes)
        spectra = dot(blocks[0], total[:, own], ((1,), (1,)))
        spectra = spectra + dot(blocks[1], swapped[:, own], ((1,), (1,)))
        spectra = spectra.reshape(MX, C, spectra.shape[1]).astype(BF16)
        pieces[:, part * C : (part + 1) * C, :] = spectra


def mode_scale(rows, local_mz):
    line = lax.broadcasted_iota(jnp.int32, (rows, 1), 0) % local_mz
    line = line + lax.axis_index("gy") * local_mz
    return jnp.where(line == 0, 1.0, 2.0).astype(F32) / float(NX * NY * NZ)


def repeat_tables():
    lane = lax.broadcasted_iota(jnp.int32, (C, C * C), 1)
    row = lax.broadcasted_iota(jnp.int32, (C, C * C), 0)
    outer = (lane // C == row).astype(F32)
    inner = (lane % C == row).astype(F32)
    return outer, inner


def mode_products(arrived, weights, spectrum, grad_hat):
    total = add_up(arrived).astype(BF16)
    spectrum[...] = total
    modes = total.shape[1] // 2
    outer, inner = repeat_tables()
    grads = dot(total[C:], inner.astype(BF16), ((0,), (0,)))
    scale = mode_scale(modes, modes // MY)
    real_d = grads[:modes] * scale
    imag_d = grads[modes:] * scale
    real_w = weights[0, 0].astype(F32).reshape(modes, C * C)
    imag_w = weights[1, 0].astype(F32).reshape(modes, C * C)
    products = jnp.concatenate(
        [real_w * real_d + imag_w * imag_d, real_w * imag_d - imag_w * real_d], axis=0
    )
    values = dot(outer, products, ((1,), (1,)), HIGHEST).astype(BF16)
    grad_hat[...] = jnp.broadcast_to(values[None], grad_hat.shape)


def weight_grads(own, other, result):
    modes = own.shape[1] // 2
    outer, inner = repeat_tables()
    outer = outer.astype(BF16)
    inner = inner.astype(BF16)
    scale = mode_scale(modes, modes // MY)
    real_sum = jnp.zeros((modes, C * C), F32)
    imag_sum = jnp.zeros((modes, C * C), F32)
    for spectrum in (own, other):
        values = spectrum[...]
        field = dot(values[:C], outer, ((0,), (0,)))
        grads = dot(values[C:], inner, ((0,), (0,)))
        real_u, imag_u = field[:modes], field[modes:]
        real_d, imag_d = grads[:modes] * scale, grads[modes:] * scale
        real_sum = real_sum + (real_u * real_d + imag_u * imag_d)
        imag_sum = imag_sum + (real_u * imag_d - imag_u * real_d)
    for part, total in enumerate((real_sum, imag_sum)):
        result[part, 0] = total.reshape(result.shape[2:])


def inverse_x(arrived, x_rows, result):
    blocks = x_blocks(x_rows)
    values = arrived[...].reshape(MX * C, arrived.shape[2])
    half = values.shape[1] // 2
    swapped = jnp.concatenate([-values[:, half:], values[:, :half]], axis=1)
    sums = dot(values, blocks[0], ((0,), (0,))) + dot(swapped, blocks[1], ((0,), (0,)))
    result[0] = sums.astype(BF16)


def inverse_yz(
    own, taken, grad_pre, z_table, y_tables, point, result, lines, staged, sems
):
    y_table = y_tables[lax.axis_index("gy")]
    rows = staged.shape[0]
    local_x = rows // C
    row = lax.broadcasted_iota(jnp.int32, (rows, C), 0) // local_x
    pick = (row == lax.broadcasted_iota(jnp.int32, (rows, C), 1)).astype(BF16)
    spread = dot(pick, point[...], ((1,), (0,))).astype(BF16)
    spread = dot(spread, pick, ((1,), (1,)))
    left = lax.broadcasted_iota(jnp.int32, (rows, rows), 0) % local_x
    right = lax.broadcasted_iota(jnp.int32, (rows, rows), 1) % local_x
    mixing = jnp.where(left == right, spread, 0.0).astype(BF16)
    side = lax.axis_index("gy") % 2
    per = MZ // own.shape[0]
    for index in range(own.shape[0]):
        for spectra, offset in ((own, side), (taken, 1 - side)):
            block = dot(y_table, spectra[index], ((0,), (0,)))
            first = (2 * index + offset) * per
            lines[pl.ds(first, per)] = block.reshape(per, -1, rows)
    width = z_table.shape[1]
    copies = []
    for group in range(result.shape[1] // width):
        block = lines[:, group * GROUP : (group + 1) * GROUP, :]
        block = block.reshape(2 * MZ * GROUP, rows).astype(BF16)
        spectral = dot(block, z_table[...], ((0,), (0,)))
        part = slice(group * width, (group + 1) * width)
        mixed = dot(mixing, grad_pre[:, part], ((1,), (0,)))
        staged[:, part] = (spectral + mixed).astype(BF16)
        copy = pltpu.make_async_copy(
            staged.at[:, pl.ds(group * width, width)],
            result.at[:, pl.ds(group * width, width)],
            sems.at[group],
        )
        copy.start()
        copies.append(copy)
    for copy in copies:
        copy.wait()


VMEM = pl.BlockSpec(memory_space=pltpu.VMEM)
HBM = pl.BlockSpec(memory_space=pltpu.HBM)


def call(body, ins, outs, scratch=(), vmem=24):
    values = [
        pltpu.with_memory_space_constraint(value, spec.memory_space) for value, spec in ins
    ]
    specs = [spec for _, spec in ins]
    shapes = [
        pltpu.VMEM(shape, dtype) if spec is VMEM else jax.ShapeDtypeStruct(shape, dtype)
        for shape, dtype, spec in outs
    ]
    return pl.pallas_call(
        body,
        in_specs=specs,
        out_specs=[spec for _, _, spec in outs],
        out_shape=shapes,
        scratch_shapes=list(scratch),
        compiler_params=pltpu.CompilerParams(vmem_limit_bytes=vmem << 20),
    )(*values)


def run_forward_zy(fields, pre_act, cotangent, z_table, y_table, local_mz):
    rows, local_yz = fields.shape
    local_y = local_yz // NZ
    modes = MY * local_mz
    half = (MZ // local_mz // 2, 2 * modes, 2 * rows)
    whole = (rows, local_yz)
    dma = pltpu.SemaphoreType.DMA
    return call(
        forward_zy,
        [(fields, HBM), (pre_act, HBM), (cotangent, HBM), (z_table, HBM), (y_table, HBM)],
        [(whole, BF16, VMEM), (half, BF16, VMEM), (half, BF16, VMEM)],
        [pltpu.VMEM(whole, BF16)] * 3
        + [
            pltpu.VMEM(z_table.shape, BF16),
            pltpu.VMEM(y_table.shape[1:], BF16),
            pltpu.VMEM((2 * MZ, local_y, 2 * rows), BF16),
            dma((3, 2)),
            dma((2,)),
        ],
    )


def run_inverse_yz(own, taken, grad_pre, z_table, y_table, point_weight):
    rows, local_yz = grad_pre.shape
    local_y = local_yz // NZ
    groups = local_y // GROUP
    (grad_fields,) = call(
        inverse_yz,
        [
            (own, VMEM),
            (taken, VMEM),
            (grad_pre, VMEM),
            (z_table, VMEM),
            (y_table, VMEM),
            (point_weight, VMEM),
        ],
        [((rows, local_yz), BF16, HBM)],
        [
            pltpu.VMEM((2 * MZ, local_y, rows), F32),
            pltpu.VMEM((rows, local_yz), BF16),
            pltpu.SemaphoreType.DMA((groups,)),
        ],
    )
    return grad_fields


def swap(values, axis, bit):
    return lax.ppermute(values, axis, [(i, i ^ bit) for i in range(lax.axis_size(axis))])


def exchange(pieces, axis):
    return lax.all_to_all(pieces, axis, split_axis=0, concat_axis=0, tiled=True)


def on_device(fields, pre_act, cotangent, spec_weight, point_weight):
    count_x = lax.axis_size("gx")
    count_y = lax.axis_size("gy")
    _, channels, local_x, local_yz = fields.shape
    local_y = local_yz // NZ
    local_mz = spec_weight.shape[3]
    rows = channels * local_x
    modes = MY * local_mz
    z_table = jnp.asarray(z_block_table())
    y_table = jnp.asarray(y_block_tables(count_y, local_y, local_mz))
    x_rows = jnp.asarray(x_row_tables(count_x, local_x))
    whole = (rows, local_yz)

    grad_pre, kept, given = run_forward_zy(
        fields.reshape(whole),
        pre_act.reshape(whole),
        cotangent.reshape(whole),
        z_table,
        y_table,
        local_mz,
    )
    taken = swap(given, "gy", 1)
    for bit in (2, 4):
        half = ((kept.shape[0] // 2,) + kept.shape[1:], BF16, VMEM)
        kept, given = call(
            functools.partial(add_halves, bit),
            [(kept, VMEM), (taken, VMEM)],
            [half, half],
        )
        taken = swap(given, "gy", bit)
    (pieces,) = call(
        forward_x,
        [(kept, VMEM), (taken, VMEM), (x_rows, VMEM)],
        [((count_x, 2 * C, 2 * modes), BF16, VMEM)],
    )
    arrived = exchange(pieces, "gx")
    spectrum, pieces = call(
        mode_products,
        [(arrived, VMEM), (spec_weight, VMEM)],
        [((2 * C, 2 * modes), BF16, VMEM), ((count_x, C, 2 * modes), BF16, VMEM)],
    )
    arrived = exchange(pieces, "gx")
    other = swap(spectrum, "dp", 1)
    (grad_spec,) = call(
        weight_grads,
        [(spectrum, VMEM), (other, VMEM)],
        [(spec_weight.shape, F32, pl.BlockSpec())],
    )
    (pieces,) = call(
        inverse_x,
        [(arrived, VMEM), (x_rows, VMEM)],
        [((1, 2 * modes, rows), BF16, VMEM)],
    )
    taken = swap(pieces, "gy", 4)
    for bit in (4, 2):
        (pieces,) = call(
            functools.partial(join_halves, bit),
            [(pieces, VMEM), (taken, VMEM)],
            [((2 * pieces.shape[0],) + pieces.shape[1:], BF16, VMEM)],
        )
        taken = swap(pieces, "gy", bit // 2)
    grad_fields = run_inverse_yz(pieces, taken, grad_pre, z_table, y_table, point_weight)
    return grad_fields.reshape(fields.shape), grad_spec


def solution(mesh):
    placed = (
        P("dp", None, "gx", "gy"),
        P("dp", None, "gx", "gy"),
        P("dp", None, "gx", "gy"),
        P(None, "gx", None, "gy", None),
        P(),
    )

    return jax.shard_map(
        on_device,
        mesh=mesh,
        in_specs=placed,
        out_specs=(P("dp", None, "gx", "gy"), P(None, "gx", None, "gy", None)),
        check_vma=False,
    )
```

```python
import math

import jax
import jax.numpy as jnp
import numpy as np
from jax import lax
from jax.experimental import pallas as pl
from jax.experimental.pallas import tpu as pltpu
from jax.sharding import PartitionSpec as P

C = 16
NX = 256
NY = 512
NZ = 64
MX = 32
MY = 32
MZ = 16
GROUP = 8

F32 = jnp.float32
BF16 = jnp.bfloat16


def signed_freqs(kept, length):
    index = np.arange(kept)
    return np.where(index < kept // 2, index, length - kept + index)


def cos_sin(freqs, points, length):
    turns = points[:, None] * freqs[None, :] % length
    angle = turns.astype(np.float32) * np.float32(2.0 * math.pi / length)
    return np.cos(angle).astype(np.float32), np.sin(angle).astype(np.float32)


def z_block_table():
    cosine, sine = cos_sin(np.arange(MZ), np.arange(NZ), NZ)
    parts = np.stack([cosine.T, -sine.T], axis=1)
    same = np.eye(GROUP, dtype=np.float32)
    table = parts[:, :, None, None, :] * same[None, None, :, :, None]
    return table.reshape(2 * MZ * GROUP, GROUP * NZ).astype(BF16)


def y_block_tables(count, local_y, local_mz):
    cosine, sine = cos_sin(signed_freqs(MY, NY), np.arange(NY), NY)
    upper = np.stack([cosine, sine], axis=-1)
    lower = np.stack([-sine, cosine], axis=-1)
    table = np.stack([upper, lower], axis=0)
    table = table.reshape(2, count, local_y, MY, 2).transpose(1, 0, 3, 4, 2)
    same = np.eye(local_mz, dtype=np.float32)
    table = table[:, :, :, None, None, :, :] * same[None, None, None, :, :, None, None]
    return table.reshape(count, 2 * MY * local_mz, local_mz * 2 * local_y).astype(BF16)


def x_row_tables(count, local_x):
    cosine, sine = cos_sin(signed_freqs(MX, NX), np.arange(NX), NX)
    table = np.stack([cosine, sine], axis=0).reshape(2, count, local_x, MX)
    table = table.transpose(1, 0, 3, 2)
    return np.tile(table, (1, 1, 1, 128 // local_x)).astype(BF16)


def dot(left, right, dims):
    return lax.dot_general(left, right, (dims, ((), ())), preferred_element_type=F32)


def gelu_slope(value):
    cdf = 0.5 * (1.0 + lax.erf(value * (1.0 / math.sqrt(2.0))))
    return cdf + value * jnp.exp(-0.5 * value * value) * (1.0 / math.sqrt(2.0 * math.pi))


def copies_in(sources, targets, sems):
    width = targets[0].shape[1] // sems.shape[1]
    copies = []
    for chunk in range(sems.shape[1]):
        lanes = pl.ds(chunk * width, width)
        copies.append(
            [
                pltpu.make_async_copy(
                    source.at[:, lanes], target.at[:, lanes], sems.at[index, chunk]
                )
                for index, (source, target) in enumerate(zip(sources, targets))
            ]
        )
    return copies


def forward_zy(
    fields, pre_act, cotangent, z_source, y_source, grad_pre, kept, given,
    fields_in, pre_in, cotangent_in, z_table, y_table, lines, sems, table_sems,
):
    groups = pre_act.shape[1] // z_source.shape[1]
    per_chunk = groups // sems.shape[1]
    tables = [
        pltpu.make_async_copy(z_source, z_table, table_sems.at[0]),
        pltpu.make_async_copy(y_source.at[lax.axis_index("gy")], y_table, table_sems.at[1]),
    ]
    copies = copies_in(
        (pre_act, cotangent, fields), (pre_in, cotangent_in, fields_in), sems
    )
    for copy in copies[0] + tables[:1]:
        copy.start()
    for chunk in copies[1:]:
        for copy in chunk:
            copy.start()
    tables[1].start()
    width = pre_in.shape[1] // groups
    pair = []
    for group in range(groups):
        if group % per_chunk == 0:
            for copy in copies[group // per_chunk]:
                copy.wait()
        part = slice(group * width, (group + 1) * width)
        slope = gelu_slope(pre_in[:, part].astype(F32))
        grad = (cotangent_in[:, part].astype(F32) * slope).astype(BF16)
        grad_pre[:, part] = grad
        both = jnp.concatenate([fields_in[:, part], grad], axis=0)
        if group == 0:
            tables[0].wait()
        spectra = dot(z_table[...], both, ((1,), (1,)))
        pair.append(spectra.reshape(2 * MZ, GROUP, both.shape[0]))
        if len(pair) == 2:
            rows = slice((group - 1) * GROUP, (group + 1) * GROUP)
            lines[:, rows, :] = jnp.concatenate(pair, axis=1).astype(BF16)
            pair = []
    tables[1].wait()
    side = lax.axis_index("gy") % 2
    count = 2 * kept.shape[0]
    per = 2 * MZ // count
    for index in range(count // 2):
        for pieces, offset in ((given, 1 - side), (kept, side)):
            first = (2 * index + offset) * per
            block = lines[pl.ds(first, per)]
            block = block.reshape(per * block.shape[1], block.shape[2])
            pieces[index] = dot(y_table[...], block, ((1,), (0,))).astype(BF16)


def add_halves(kept, taken, sums):
    sums[...] = (kept[...].astype(F32) + taken[...].astype(F32)).astype(BF16)


def add_up(arrived):
    total = arrived[0].astype(F32)
    for index in range(1, arrived.shape[0]):
        total = total + arrived[index].astype(F32)
    return total


def x_blocks(x_rows):
    lanes = x_rows.shape[3]
    owner = lax.broadcasted_iota(jnp.int32, (C, lanes), 1) // (lanes // C)
    mask = owner == lax.broadcasted_iota(jnp.int32, (C, lanes), 0)
    rows = x_rows[lax.axis_index("gx")].astype(F32)
    blocks = []
    for part in range(2):
        table = jnp.where(mask[None], rows[part][:, None, :], 0.0)
        blocks.append(table.reshape(MX * C, lanes).astype(BF16))
    return blocks


def forward_x(arrived, x_rows, pieces):
    blocks = x_blocks(x_rows)
    total = add_up(arrived)
    half = total.shape[0] // 2
    swapped = jnp.concatenate([total[half:], -total[:half]], axis=0).astype(BF16)
    total = total.astype(BF16)
    lanes = blocks[0].shape[1]
    for part in range(2):
        own = slice(part * lanes, (part + 1) * lanes)
        spectra = dot(blocks[0], total[:, own], ((1,), (1,)))
        spectra = spectra + dot(blocks[1], swapped[:, own], ((1,), (1,)))
        spectra = spectra.reshape(MX, C, spectra.shape[1]).astype(BF16)
        pieces[:, part * C : (part + 1) * C, :] = spectra


def mode_scale(rows, local_mz):
    line = lax.broadcasted_iota(jnp.int32, (rows, 1), 0) % local_mz
    line = line + lax.axis_index("gy") * local_mz
    return jnp.where(line == 0, 1.0, 2.0).astype(F32) / float(NX * NY * NZ)


def repeat_tables():
    lane = lax.broadcasted_iota(jnp.int32, (C, C * C), 1)
    row = lax.broadcasted_iota(jnp.int32, (C, C * C), 0)
    outer = (lane // C == row).astype(F32)
    inner = (lane % C == row).astype(F32)
    return outer, inner


def mode_products(arrived, weights, spectrum, grad_hat):
    total = add_up(arrived).astype(BF16)
    spectrum[...] = total
    modes = total.shape[1] // 2
    outer, inner = repeat_tables()
    grads = dot(total[C:], inner.astype(BF16), ((0,), (0,)))
    scale = mode_scale(modes, modes // MY)
    real_d = grads[:modes] * scale
    imag_d = grads[modes:] * scale
    real_w = weights[0, 0].astype(F32).reshape(modes, C * C)
    imag_w = weights[1, 0].astype(F32).reshape(modes, C * C)
    products = jnp.concatenate(
        [real_w * real_d + imag_w * imag_d, real_w * imag_d - imag_w * real_d], axis=0
    )
    values = None
    for _ in range(3):
        piece = products.astype(BF16)
        products = products - piece.astype(F32)
        term = dot(outer.astype(BF16), piece, ((1,), (1,)))
        values = term if values is None else values + term
    values = values.astype(BF16)
    grad_hat[...] = jnp.broadcast_to(values[None], grad_hat.shape)


def weight_grads(own, other, result):
    modes = own.shape[1] // 2
    outer, inner = repeat_tables()
    outer = outer.astype(BF16)
    inner = inner.astype(BF16)
    scale = mode_scale(modes, modes // MY)
    real_sum = jnp.zeros((modes, C * C), F32)
    imag_sum = jnp.zeros((modes, C * C), F32)
    for spectrum in (own, other):
        values = spectrum[...]
        field = dot(values[:C], outer, ((0,), (0,)))
        grads = dot(values[C:], inner, ((0,), (0,)))
        real_u, imag_u = field[:modes], field[modes:]
        real_d, imag_d = grads[:modes] * scale, grads[modes:] * scale
        real_sum = real_sum + (real_u * real_d + imag_u * imag_d)
        imag_sum = imag_sum + (real_u * imag_d - imag_u * real_d)
    for part, total in enumerate((real_sum, imag_sum)):
        result[part, 0] = total.reshape(result.shape[2:])


def inverse_x(arrived, x_rows, result):
    blocks = x_blocks(x_rows)
    values = arrived[...].reshape(MX * C, arrived.shape[2])
    half = values.shape[1] // 2
    swapped = jnp.concatenate([-values[:, half:], values[:, :half]], axis=1)
    sums = dot(values, blocks[0], ((0,), (0,))) + dot(swapped, blocks[1], ((0,), (0,)))
    result[...] = jnp.broadcast_to(sums.astype(BF16)[None], result.shape)


def inverse_yz(
    arrived, grad_pre, z_table, y_tables, point, result, lines, staged, sems
):
    y_table = y_tables[lax.axis_index("gy")]
    rows = staged.shape[0]
    local_x = rows // C
    row = lax.broadcasted_iota(jnp.int32, (rows, C), 0) // local_x
    pick = (row == lax.broadcasted_iota(jnp.int32, (rows, C), 1)).astype(BF16)
    spread = dot(pick, point[...], ((1,), (0,))).astype(BF16)
    spread = dot(spread, pick, ((1,), (1,)))
    left = lax.broadcasted_iota(jnp.int32, (rows, rows), 0) % local_x
    right = lax.broadcasted_iota(jnp.int32, (rows, rows), 1) % local_x
    mixing = jnp.where(left == right, spread, 0.0).astype(BF16)
    count = arrived.shape[0]
    per = 2 * MZ // count
    for index in range(count):
        block = dot(y_table, arrived[index], ((0,), (0,)))
        lines[index * per : (index + 1) * per] = block.reshape(per, -1, rows)
    width = z_table.shape[1]
    copies = []
    for group in range(result.shape[1] // width):
        block = lines[:, group * GROUP : (group + 1) * GROUP, :]
        block = block.reshape(2 * MZ * GROUP, rows).astype(BF16)
        spectral = dot(block, z_table[...], ((0,), (0,)))
        part = slice(group * width, (group + 1) * width)
        mixed = dot(mixing, grad_pre[:, part], ((1,), (0,)))
        staged[:, part] = (spectral + mixed).astype(BF16)
        copy = pltpu.make_async_copy(
            staged.at[:, pl.ds(group * width, width)],
            result.at[:, pl.ds(group * width, width)],
            sems.at[group],
        )
        copy.start()
        copies.append(copy)
    for copy in copies:
        copy.wait()


VMEM = pl.BlockSpec(memory_space=pltpu.VMEM)
HBM = pl.BlockSpec(memory_space=pltpu.HBM)


def call(body, ins, outs, scratch=(), vmem=24):
    values = [
        pltpu.with_memory_space_constraint(value, spec.memory_space) for value, spec in ins
    ]
    specs = [spec for _, spec in ins]
    shapes = [
        pltpu.VMEM(shape, dtype) if spec is VMEM else jax.ShapeDtypeStruct(shape, dtype)
        for shape, dtype, spec in outs
    ]
    return pl.pallas_call(
        body,
        in_specs=specs,
        out_specs=[spec for _, _, spec in outs],
        out_shape=shapes,
        scratch_shapes=list(scratch),
        compiler_params=pltpu.CompilerParams(vmem_limit_bytes=vmem << 20),
    )(*values)


def run_forward_zy(fields, pre_act, cotangent, z_table, y_table, local_mz):
    rows, local_yz = fields.shape
    local_y = local_yz // NZ
    modes = MY * local_mz
    half = (MZ // local_mz // 2, 2 * modes, 2 * rows)
    whole = (rows, local_yz)
    dma = pltpu.SemaphoreType.DMA
    return call(
        forward_zy,
        [(fields, HBM), (pre_act, HBM), (cotangent, HBM), (z_table, HBM), (y_table, HBM)],
        [(whole, BF16, VMEM), (half, BF16, VMEM), (half, BF16, VMEM)],
        [pltpu.VMEM(whole, BF16)] * 3
        + [
            pltpu.VMEM(z_table.shape, BF16),
            pltpu.VMEM(y_table.shape[1:], BF16),
            pltpu.VMEM((2 * MZ, local_y, 2 * rows), BF16),
            dma((3, 2)),
            dma((2,)),
        ],
    )


def run_inverse_yz(arrived, grad_pre, z_table, y_table, point_weight):
    rows, local_yz = grad_pre.shape
    local_y = local_yz // NZ
    groups = local_y // GROUP
    (grad_fields,) = call(
        inverse_yz,
        [
            (arrived, VMEM),
            (grad_pre, VMEM),
            (z_table, VMEM),
            (y_table, VMEM),
            (point_weight, VMEM),
        ],
        [((rows, local_yz), BF16, HBM)],
        [
            pltpu.VMEM((2 * MZ, local_y, rows), F32),
            pltpu.VMEM((rows, local_yz), BF16),
            pltpu.SemaphoreType.DMA((groups,)),
        ],
    )
    return grad_fields


def exchange(pieces, axis, groups=None):
    return lax.all_to_all(
        pieces, axis, split_axis=0, concat_axis=0, tiled=True, axis_index_groups=groups
    )


def on_device(fields, pre_act, cotangent, spec_weight, point_weight):
    count_x = lax.axis_size("gx")
    count_y = lax.axis_size("gy")
    _, channels, local_x, local_yz = fields.shape
    local_y = local_yz // NZ
    local_mz = spec_weight.shape[3]
    rows = channels * local_x
    modes = MY * local_mz
    z_table = jnp.asarray(z_block_table())
    y_table = jnp.asarray(y_block_tables(count_y, local_y, local_mz))
    x_rows = jnp.asarray(x_row_tables(count_x, local_x))
    whole = (rows, local_yz)

    grad_pre, kept, given = run_forward_zy(
        fields.reshape(whole),
        pre_act.reshape(whole),
        cotangent.reshape(whole),
        z_table,
        y_table,
        local_mz,
    )
    taken = lax.ppermute(given, "gy", [(i, i ^ 1) for i in range(count_y)])
    (sums,) = call(add_halves, [(kept, VMEM), (taken, VMEM)], [(kept.shape, BF16, VMEM)])
    sides = [list(range(side, count_y, 2)) for side in range(2)]
    arrived = exchange(sums, "gy", sides)
    (pieces,) = call(
        forward_x,
        [(arrived, VMEM), (x_rows, VMEM)],
        [((count_x, 2 * C, 2 * modes), BF16, VMEM)],
    )
    arrived = exchange(pieces, "gx")
    spectrum, pieces = call(
        mode_products,
        [(arrived, VMEM), (spec_weight, VMEM)],
        [((2 * C, 2 * modes), BF16, VMEM), ((count_x, C, 2 * modes), BF16, VMEM)],
    )
    arrived = exchange(pieces, "gx")
    other = lax.ppermute(spectrum, "dp", [(0, 1), (1, 0)])
    (grad_spec,) = call(
        weight_grads,
        [(spectrum, VMEM), (other, VMEM)],
        [(spec_weight.shape, F32, pl.BlockSpec())],
    )
    (pieces,) = call(
        inverse_x,
        [(arrived, VMEM), (x_rows, VMEM)],
        [((count_y, 2 * modes, rows), BF16, VMEM)],
    )
    arrived = exchange(pieces, "gy")
    grad_fields = run_inverse_yz(arrived, grad_pre, z_table, y_table, point_weight)
    return grad_fields.reshape(fields.shape), grad_spec


def solution(mesh):
    placed = (
        P("dp", None, "gx", "gy"),
        P("dp", None, "gx", "gy"),
        P("dp", None, "gx", "gy"),
        P(None, "gx", None, "gy", None),
        P(),
    )

    return jax.shard_map(
        on_device,
        mesh=mesh,
        in_specs=placed,
        out_specs=(P("dp", None, "gx", "gy"), P(None, "gx", None, "gy", None)),
        check_vma=False,
    )
```

```python
import math

import jax
import jax.numpy as jnp
import numpy as np
from jax import lax
from jax.experimental import pallas as pl
from jax.experimental.pallas import tpu as pltpu
from jax.sharding import PartitionSpec as P

C = 16
NX = 256
NY = 512
NZ = 64
MX = 32
MY = 32
MZ = 16
GROUP = 8

F32 = jnp.float32
BF16 = jnp.bfloat16


def signed_freqs(kept, length):
    index = np.arange(kept)
    return np.where(index < kept // 2, index, length - kept + index)


def cos_sin(freqs, points, length):
    turns = points[:, None] * freqs[None, :] % length
    angle = turns.astype(np.float32) * np.float32(2.0 * math.pi / length)
    return np.cos(angle).astype(np.float32), np.sin(angle).astype(np.float32)


def z_block_table():
    cosine, sine = cos_sin(np.arange(MZ), np.arange(NZ), NZ)
    parts = np.stack([cosine.T, -sine.T], axis=1)
    same = np.eye(GROUP, dtype=np.float32)
    table = parts[:, :, None, None, :] * same[None, None, :, :, None]
    return table.reshape(2 * MZ * GROUP, GROUP * NZ).astype(BF16)


def y_block_tables(count, local_y, local_mz):
    cosine, sine = cos_sin(signed_freqs(MY, NY), np.arange(NY), NY)
    upper = np.stack([cosine, sine], axis=-1)
    lower = np.stack([-sine, cosine], axis=-1)
    table = np.stack([upper, lower], axis=0)
    table = table.reshape(2, count, local_y, MY, 2).transpose(1, 0, 3, 4, 2)
    same = np.eye(local_mz, dtype=np.float32)
    table = table[:, :, :, None, None, :, :] * same[None, None, None, :, :, None, None]
    return table.reshape(count, 2 * MY * local_mz, local_mz * 2 * local_y).astype(BF16)


def x_row_tables(count, local_x):
    cosine, sine = cos_sin(signed_freqs(MX, NX), np.arange(NX), NX)
    table = np.stack([cosine, sine], axis=0).reshape(2, count, local_x, MX)
    table = table.transpose(1, 0, 3, 2)
    return np.tile(table, (1, 1, 1, 128 // local_x)).astype(BF16)


def dot(left, right, dims):
    return lax.dot_general(left, right, (dims, ((), ())), preferred_element_type=F32)


def gelu_slope(value):
    cdf = 0.5 * (1.0 + lax.erf(value * (1.0 / math.sqrt(2.0))))
    return cdf + value * jnp.exp(-0.5 * value * value) * (1.0 / math.sqrt(2.0 * math.pi))


def copies_in(sources, targets, sems):
    width = targets[0].shape[1] // sems.shape[1]
    copies = []
    for chunk in range(sems.shape[1]):
        lanes = pl.ds(chunk * width, width)
        copies.append(
            [
                pltpu.make_async_copy(
                    source.at[:, lanes], target.at[:, lanes], sems.at[index, chunk]
                )
                for index, (source, target) in enumerate(zip(sources, targets))
            ]
        )
    return copies


def forward_zy(
    fields, pre_act, cotangent, z_source, y_source, grad_pre, kept, given,
    fields_in, pre_in, cotangent_in, z_table, y_table, lines, sems, table_sems,
):
    groups = pre_act.shape[1] // z_source.shape[1]
    per_chunk = groups // sems.shape[1]
    tables = [
        pltpu.make_async_copy(z_source, z_table, table_sems.at[0]),
        pltpu.make_async_copy(y_source.at[lax.axis_index("gy")], y_table, table_sems.at[1]),
    ]
    copies = copies_in(
        (pre_act, cotangent, fields), (pre_in, cotangent_in, fields_in), sems
    )
    for copy in copies[0] + tables[:1]:
        copy.start()
    for chunk in copies[1:]:
        for copy in chunk:
            copy.start()
    tables[1].start()
    width = pre_in.shape[1] // groups
    pair = []
    for group in range(groups):
        if group % per_chunk == 0:
            for copy in copies[group // per_chunk]:
                copy.wait()
        part = slice(group * width, (group + 1) * width)
        slope = gelu_slope(pre_in[:, part].astype(F32))
        grad = (cotangent_in[:, part].astype(F32) * slope).astype(BF16)
        grad_pre[:, part] = grad
        both = jnp.concatenate([fields_in[:, part], grad], axis=0)
        if group == 0:
            tables[0].wait()
        spectra = dot(z_table[...], both, ((1,), (1,)))
        pair.append(spectra.reshape(2 * MZ, GROUP, both.shape[0]))
        if len(pair) == 2:
            rows = slice((group - 1) * GROUP, (group + 1) * GROUP)
            lines[:, rows, :] = jnp.concatenate(pair, axis=1).astype(BF16)
            pair = []
    tables[1].wait()
    side = lax.axis_index("gy") % 2
    count = 2 * kept.shape[0]
    per = 2 * MZ // count
    for index in range(count // 2):
        for pieces, offset in ((given, 1 - side), (kept, side)):
            first = (2 * index + offset) * per
            block = lines[pl.ds(first, per)]
            block = block.reshape(per * block.shape[1], block.shape[2])
            pieces[index] = dot(y_table[...], block, ((1,), (0,))).astype(BF16)


def add_halves(kept, taken, sums):
    sums[...] = (kept[...].astype(F32) + taken[...].astype(F32)).astype(BF16)


def add_up(arrived):
    total = arrived[0].astype(F32)
    for index in range(1, arrived.shape[0]):
        total = total + arrived[index].astype(F32)
    return total


def x_blocks(x_rows):
    lanes = x_rows.shape[3]
    owner = lax.broadcasted_iota(jnp.int32, (C, lanes), 1) // (lanes // C)
    mask = owner == lax.broadcasted_iota(jnp.int32, (C, lanes), 0)
    rows = x_rows[lax.axis_index("gx")].astype(F32)
    blocks = []
    for part in range(2):
        table = jnp.where(mask[None], rows[part][:, None, :], 0.0)
        blocks.append(table.reshape(MX * C, lanes).astype(BF16))
    return blocks


def forward_x(arrived, x_rows, pieces):
    blocks = x_blocks(x_rows)
    total = add_up(arrived)
    half = total.shape[0] // 2
    swapped = jnp.concatenate([total[half:], -total[:half]], axis=0).astype(BF16)
    total = total.astype(BF16)
    lanes = blocks[0].shape[1]
    for part in range(2):
        own = slice(part * lanes, (part + 1) * lanes)
        spectra = dot(blocks[0], total[:, own], ((1,), (1,)))
        spectra = spectra + dot(blocks[1], swapped[:, own], ((1,), (1,)))
        spectra = spectra.reshape(MX, C, spectra.shape[1]).astype(BF16)
        pieces[:, part * C : (part + 1) * C, :] = spectra


def mode_scale(rows, local_mz):
    line = lax.broadcasted_iota(jnp.int32, (rows, 1), 0) % local_mz
    line = line + lax.axis_index("gy") * local_mz
    return jnp.where(line == 0, 1.0, 2.0).astype(F32) / float(NX * NY * NZ)


def repeat_tables():
    lane = lax.broadcasted_iota(jnp.int32, (C, C * C), 1)
    row = lax.broadcasted_iota(jnp.int32, (C, C * C), 0)
    outer = (lane // C == row).astype(F32)
    inner = (lane % C == row).astype(F32)
    return outer, inner


def mode_products(arrived, weights, spectrum, grad_hat):
    total = add_up(arrived).astype(BF16)
    spectrum[...] = total
    modes = total.shape[1] // 2
    outer, inner = repeat_tables()
    grads = dot(total[C:], inner.astype(BF16), ((0,), (0,)))
    scale = mode_scale(modes, modes // MY)
    real_d = grads[:modes] * scale
    imag_d = grads[modes:] * scale
    real_w = weights[0, 0].astype(F32).reshape(modes, C * C)
    imag_w = weights[1, 0].astype(F32).reshape(modes, C * C)
    products = jnp.concatenate(
        [real_w * real_d + imag_w * imag_d, real_w * imag_d - imag_w * real_d], axis=0
    )
    values = None
    for _ in range(3):
        piece = products.astype(BF16)
        products = products - piece.astype(F32)
        term = dot(outer.astype(BF16), piece, ((1,), (1,)))
        values = term if values is None else values + term
    values = values.astype(BF16)
    grad_hat[...] = jnp.broadcast_to(values[None], grad_hat.shape)


def weight_grads(both, result):
    modes = both.shape[2] // 2
    outer, inner = repeat_tables()
    outer = outer.astype(BF16)
    inner = inner.astype(BF16)
    scale = mode_scale(modes, modes // MY)
    real_sum = jnp.zeros((modes, C * C), F32)
    imag_sum = jnp.zeros((modes, C * C), F32)
    for sample in range(both.shape[0]):
        values = both[sample]
        field = dot(values[:C], outer, ((0,), (0,)))
        grads = dot(values[C:], inner, ((0,), (0,)))
        real_u, imag_u = field[:modes], field[modes:]
        real_d, imag_d = grads[:modes] * scale, grads[modes:] * scale
        real_sum = real_sum + (real_u * real_d + imag_u * imag_d)
        imag_sum = imag_sum + (real_u * imag_d - imag_u * real_d)
    for part, total in enumerate((real_sum, imag_sum)):
        result[part, 0] = total.reshape(result.shape[2:])


def pair_spectra(own, other, both):
    both[0] = own[...]
    both[1] = other[...]


def inverse_x(arrived, x_rows, result):
    blocks = x_blocks(x_rows)
    values = arrived[...].reshape(MX * C, arrived.shape[2])
    half = values.shape[1] // 2
    swapped = jnp.concatenate([-values[:, half:], values[:, :half]], axis=1)
    sums = dot(values, blocks[0], ((0,), (0,))) + dot(swapped, blocks[1], ((0,), (0,)))
    result[...] = jnp.broadcast_to(sums.astype(BF16)[None], result.shape)


def mixing_table(point, rows):
    local_x = rows // C
    row = lax.broadcasted_iota(jnp.int32, (rows, C), 0) // local_x
    pick = (row == lax.broadcasted_iota(jnp.int32, (rows, C), 1)).astype(BF16)
    spread = dot(pick, point[...], ((1,), (0,))).astype(BF16)
    spread = dot(spread, pick, ((1,), (1,)))
    left = lax.broadcasted_iota(jnp.int32, (rows, rows), 0) % local_x
    right = lax.broadcasted_iota(jnp.int32, (rows, rows), 1) % local_x
    return jnp.where(left == right, spread, 0.0).astype(BF16)


def inverse_yz(
    own, taken, grad_pre, z_table, y_tables, point, both, result, grad_spec,
    lines, staged, spec_staged, sems, spec_sem,
):
    y_table = y_tables[lax.axis_index("gy")]
    rows = staged.shape[0]
    mixing = mixing_table(point, rows)
    side = lax.axis_index("gy") % 2
    per = MZ // own.shape[0]
    for index in range(own.shape[0]):
        for spectra, offset in ((own, side), (taken, 1 - side)):
            block = dot(y_table, spectra[index], ((0,), (0,)))
            first = (2 * index + offset) * per
            lines[pl.ds(first, per)] = block.reshape(per, -1, rows)
    weight_grads(both, spec_staged)
    spec_copy = pltpu.make_async_copy(spec_staged, grad_spec, spec_sem)
    spec_copy.start()
    width = z_table.shape[1]
    copies = [spec_copy]
    for group in range(result.shape[1] // width):
        block = lines[:, group * GROUP : (group + 1) * GROUP, :]
        block = block.reshape(2 * MZ * GROUP, rows).astype(BF16)
        part = slice(group * width, (group + 1) * width)
        spectral = dot(block, z_table[...], ((0,), (0,)))
        mixed = dot(mixing, grad_pre[:, part], ((1,), (0,)))
        staged[:, part] = (spectral + mixed).astype(BF16)
        copy = pltpu.make_async_copy(
            staged.at[:, pl.ds(group * width, width)],
            result.at[:, pl.ds(group * width, width)],
            sems.at[group],
        )
        copy.start()
        copies.append(copy)
    for copy in copies:
        copy.wait()


VMEM = pl.BlockSpec(memory_space=pltpu.VMEM)
HBM = pl.BlockSpec(memory_space=pltpu.HBM)


def call(body, ins, outs, scratch=(), vmem=24):
    values = [
        pltpu.with_memory_space_constraint(value, spec.memory_space) for value, spec in ins
    ]
    specs = [spec for _, spec in ins]
    shapes = [
        pltpu.VMEM(shape, dtype) if spec is VMEM else jax.ShapeDtypeStruct(shape, dtype)
        for shape, dtype, spec in outs
    ]
    return pl.pallas_call(
        body,
        in_specs=specs,
        out_specs=[spec for _, _, spec in outs],
        out_shape=shapes,
        scratch_shapes=list(scratch),
        compiler_params=pltpu.CompilerParams(vmem_limit_bytes=vmem << 20),
    )(*values)


def run_forward_zy(fields, pre_act, cotangent, z_table, y_table, local_mz):
    rows, local_yz = fields.shape
    local_y = local_yz // NZ
    modes = MY * local_mz
    half = (MZ // local_mz // 2, 2 * modes, 2 * rows)
    whole = (rows, local_yz)
    dma = pltpu.SemaphoreType.DMA
    return call(
        forward_zy,
        [(fields, HBM), (pre_act, HBM), (cotangent, HBM), (z_table, HBM), (y_table, HBM)],
        [(whole, BF16, VMEM), (half, BF16, VMEM), (half, BF16, VMEM)],
        [pltpu.VMEM(whole, BF16)] * 3
        + [
            pltpu.VMEM(z_table.shape, BF16),
            pltpu.VMEM(y_table.shape[1:], BF16),
            pltpu.VMEM((2 * MZ, local_y, 2 * rows), BF16),
            dma((3, 2)),
            dma((2,)),
        ],
    )


def run_inverse_yz(own, taken, grad_pre, z_table, y_table, point, both, spec_shape):
    rows, local_yz = grad_pre.shape
    local_y = local_yz // NZ
    groups = local_y // GROUP
    return call(
        inverse_yz,
        [
            (own, VMEM),
            (taken, VMEM),
            (grad_pre, VMEM),
            (z_table, VMEM),
            (y_table, VMEM),
            (point, VMEM),
            (both, VMEM),
        ],
        [((rows, local_yz), BF16, HBM), (spec_shape, F32, HBM)],
        [
            pltpu.VMEM((2 * MZ, local_y, rows), F32),
            pltpu.VMEM((rows, local_yz), BF16),
            pltpu.VMEM(spec_shape, F32),
            pltpu.SemaphoreType.DMA((groups,)),
            pltpu.SemaphoreType.DMA(()),
        ],
    )


def exchange(pieces, axis, groups=None):
    return lax.all_to_all(
        pieces, axis, split_axis=0, concat_axis=0, tiled=True, axis_index_groups=groups
    )


def on_device(fields, pre_act, cotangent, spec_weight, point_weight):
    count_x = lax.axis_size("gx")
    count_y = lax.axis_size("gy")
    _, channels, local_x, local_yz = fields.shape
    local_y = local_yz // NZ
    local_mz = spec_weight.shape[3]
    rows = channels * local_x
    modes = MY * local_mz
    z_table = jnp.asarray(z_block_table())
    y_table = jnp.asarray(y_block_tables(count_y, local_y, local_mz))
    x_rows = jnp.asarray(x_row_tables(count_x, local_x))
    whole = (rows, local_yz)

    grad_pre, kept, given = run_forward_zy(
        fields.reshape(whole),
        pre_act.reshape(whole),
        cotangent.reshape(whole),
        z_table,
        y_table,
        local_mz,
    )
    other_side = [(i, i ^ 1) for i in range(count_y)]
    taken = lax.ppermute(given, "gy", other_side)
    (sums,) = call(add_halves, [(kept, VMEM), (taken, VMEM)], [(kept.shape, BF16, VMEM)])
    sides = [list(range(side, count_y, 2)) for side in range(2)]
    arrived = exchange(sums, "gy", sides)
    (pieces,) = call(
        forward_x,
        [(arrived, VMEM), (x_rows, VMEM)],
        [((count_x, 2 * C, 2 * modes), BF16, VMEM)],
    )
    arrived = exchange(pieces, "gx")
    spectrum, pieces = call(
        mode_products,
        [(arrived, VMEM), (spec_weight, VMEM)],
        [((2 * C, 2 * modes), BF16, VMEM), ((count_x, C, 2 * modes), BF16, VMEM)],
    )
    arrived = exchange(pieces, "gx")
    other = lax.ppermute(spectrum, "dp", [(0, 1), (1, 0)])
    (both,) = call(
        pair_spectra,
        [(spectrum, VMEM), (other, VMEM)],
        [((2,) + spectrum.shape, BF16, VMEM)],
    )
    (pieces,) = call(
        inverse_x,
        [(arrived, VMEM), (x_rows, VMEM)],
        [((count_y // 2, 2 * modes, rows), BF16, VMEM)],
    )
    own = exchange(pieces, "gy", sides)
    taken = lax.ppermute(own, "gy", other_side)
    grad_fields, grad_spec = run_inverse_yz(
        own, taken, grad_pre, z_table, y_table, point_weight, both, spec_weight.shape
    )
    return grad_fields.reshape(fields.shape), grad_spec


def solution(mesh):
    placed = (
        P("dp", None, "gx", "gy"),
        P("dp", None, "gx", "gy"),
        P("dp", None, "gx", "gy"),
        P(None, "gx", None, "gy", None),
        P(),
    )

    return jax.shard_map(
        on_device,
        mesh=mesh,
        in_specs=placed,
        out_specs=(P("dp", None, "gx", "gy"), P(None, "gx", None, "gy", None)),
        check_vma=False,
    )
```

```python
import math

import jax
import jax.numpy as jnp
import numpy as np
from jax import lax
from jax.experimental import pallas as pl
from jax.experimental.pallas import tpu as pltpu
from jax.sharding import PartitionSpec as P

C = 16
NX = 256
NY = 512
NZ = 64
MX = 32
MY = 32
MZ = 16
GROUP = 8

F32 = jnp.float32
BF16 = jnp.bfloat16


def signed_freqs(kept, length):
    index = np.arange(kept)
    return np.where(index < kept // 2, index, length - kept + index)


def cos_sin(freqs, points, length):
    turns = points[:, None] * freqs[None, :] % length
    angle = turns.astype(np.float32) * np.float32(2.0 * math.pi / length)
    return np.cos(angle).astype(np.float32), np.sin(angle).astype(np.float32)


def z_block_table():
    cosine, sine = cos_sin(np.arange(MZ), np.arange(NZ), NZ)
    parts = np.stack([cosine.T, -sine.T], axis=1)
    same = np.eye(GROUP, dtype=np.float32)
    table = parts[:, :, None, None, :] * same[None, None, :, :, None]
    return table.reshape(2 * MZ * GROUP, GROUP * NZ).astype(BF16)


def y_block_tables(count, local_y, local_mz):
    cosine, sine = cos_sin(signed_freqs(MY, NY), np.arange(NY), NY)
    upper = np.stack([cosine, sine], axis=-1)
    lower = np.stack([-sine, cosine], axis=-1)
    table = np.stack([upper, lower], axis=0)
    table = table.reshape(2, count, local_y, MY, 2).transpose(1, 0, 3, 4, 2)
    same = np.eye(local_mz, dtype=np.float32)
    table = table[:, :, :, None, None, :, :] * same[None, None, None, :, :, None, None]
    return table.reshape(count, 2 * MY * local_mz, local_mz * 2 * local_y).astype(BF16)


def x_row_tables(count, local_x):
    cosine, sine = cos_sin(signed_freqs(MX, NX), np.arange(NX), NX)
    table = np.stack([cosine, sine], axis=0).reshape(2, count, local_x, MX)
    table = table.transpose(1, 0, 3, 2)
    return np.tile(table, (1, 1, 1, 128 // local_x)).astype(BF16)


def dot(left, right, dims):
    return lax.dot_general(left, right, (dims, ((), ())), preferred_element_type=F32)


def gelu_slope(value):
    cdf = 0.5 * (1.0 + lax.erf(value * (1.0 / math.sqrt(2.0))))
    return cdf + value * jnp.exp(-0.5 * value * value) * (1.0 / math.sqrt(2.0 * math.pi))


def copies_in(sources, targets, sems):
    width = targets[0].shape[1] // sems.shape[1]
    copies = []
    for chunk in range(sems.shape[1]):
        lanes = pl.ds(chunk * width, width)
        copies.append(
            [
                pltpu.make_async_copy(
                    source.at[:, lanes], target.at[:, lanes], sems.at[index, chunk]
                )
                for index, (source, target) in enumerate(zip(sources, targets))
            ]
        )
    return copies


def forward_zy(
    fields, pre_act, cotangent, z_source, y_source, grad_pre, kept, given,
    fields_in, pre_in, cotangent_in, z_table, y_table, lines, sems, table_sems,
):
    groups = pre_act.shape[1] // z_source.shape[1]
    per_chunk = groups // sems.shape[1]
    tables = [
        pltpu.make_async_copy(z_source, z_table, table_sems.at[0]),
        pltpu.make_async_copy(y_source.at[lax.axis_index("gy")], y_table, table_sems.at[1]),
    ]
    copies = copies_in(
        (pre_act, cotangent, fields), (pre_in, cotangent_in, fields_in), sems
    )
    for copy in copies[0] + tables[:1]:
        copy.start()
    for chunk in copies[1:]:
        for copy in chunk:
            copy.start()
    tables[1].start()
    width = pre_in.shape[1] // groups
    pair = []
    for group in range(groups):
        if group % per_chunk == 0:
            for copy in copies[group // per_chunk]:
                copy.wait()
        part = slice(group * width, (group + 1) * width)
        slope = gelu_slope(pre_in[:, part].astype(F32))
        grad = (cotangent_in[:, part].astype(F32) * slope).astype(BF16)
        grad_pre[:, part] = grad
        both = jnp.concatenate([fields_in[:, part], grad], axis=0)
        if group == 0:
            tables[0].wait()
        spectra = dot(z_table[...], both, ((1,), (1,)))
        pair.append(spectra.reshape(2 * MZ, GROUP, both.shape[0]))
        if len(pair) == 2:
            rows = slice((group - 1) * GROUP, (group + 1) * GROUP)
            lines[:, rows, :] = jnp.concatenate(pair, axis=1).astype(BF16)
            pair = []
    tables[1].wait()
    side = lax.axis_index("gy") % 2
    count = 2 * kept.shape[0]
    per = 2 * MZ // count
    for index in range(count // 2):
        for pieces, offset in ((given, 1 - side), (kept, side)):
            first = (2 * index + offset) * per
            block = lines[pl.ds(first, per)]
            block = block.reshape(per * block.shape[1], block.shape[2])
            pieces[index] = dot(y_table[...], block, ((1,), (0,))).astype(BF16)


def add_halves(kept, taken, sums):
    sums[...] = (kept[...].astype(F32) + taken[...].astype(F32)).astype(BF16)


def add_up(arrived):
    total = arrived[0].astype(F32)
    for index in range(1, arrived.shape[0]):
        total = total + arrived[index].astype(F32)
    return total


def x_blocks(x_rows):
    lanes = x_rows.shape[3]
    owner = lax.broadcasted_iota(jnp.int32, (C, lanes), 1) // (lanes // C)
    mask = owner == lax.broadcasted_iota(jnp.int32, (C, lanes), 0)
    rows = x_rows[lax.axis_index("gx")].astype(F32)
    blocks = []
    for part in range(2):
        table = jnp.where(mask[None], rows[part][:, None, :], 0.0)
        blocks.append(table.reshape(MX * C, lanes).astype(BF16))
    return blocks


def forward_x(arrived, x_rows, pieces):
    blocks = x_blocks(x_rows)
    total = add_up(arrived)
    half = total.shape[0] // 2
    swapped = jnp.concatenate([total[half:], -total[:half]], axis=0).astype(BF16)
    total = total.astype(BF16)
    lanes = blocks[0].shape[1]
    for part in range(2):
        own = slice(part * lanes, (part + 1) * lanes)
        spectra = dot(blocks[0], total[:, own], ((1,), (1,)))
        spectra = spectra + dot(blocks[1], swapped[:, own], ((1,), (1,)))
        spectra = spectra.reshape(MX, C, spectra.shape[1]).astype(BF16)
        pieces[:, part * C : (part + 1) * C, :] = spectra


def mode_scale(rows, local_mz):
    line = lax.broadcasted_iota(jnp.int32, (rows, 1), 0) % local_mz
    line = line + lax.axis_index("gy") * local_mz
    return jnp.where(line == 0, 1.0, 2.0).astype(F32) / float(NX * NY * NZ)


def repeat_tables():
    lane = lax.broadcasted_iota(jnp.int32, (C, C * C), 1)
    row = lax.broadcasted_iota(jnp.int32, (C, C * C), 0)
    outer = (lane // C == row).astype(F32)
    inner = (lane % C == row).astype(F32)
    return outer, inner


def mode_products(arrived, weights, spectrum, grad_hat):
    total = add_up(arrived).astype(BF16)
    spectrum[...] = total
    modes = total.shape[1] // 2
    outer, inner = repeat_tables()
    grads = dot(total[C:], inner.astype(BF16), ((0,), (0,)))
    scale = mode_scale(modes, modes // MY)
    real_d = grads[:modes] * scale
    imag_d = grads[modes:] * scale
    real_w = weights[0, 0].astype(F32).reshape(modes, C * C)
    imag_w = weights[1, 0].astype(F32).reshape(modes, C * C)
    products = jnp.concatenate(
        [real_w * real_d + imag_w * imag_d, real_w * imag_d - imag_w * real_d], axis=0
    )
    values = None
    for _ in range(3):
        piece = products.astype(BF16)
        products = products - piece.astype(F32)
        term = dot(outer.astype(BF16), piece, ((1,), (1,)))
        values = term if values is None else values + term
    values = values.astype(BF16)
    grad_hat[...] = jnp.broadcast_to(values[None], grad_hat.shape)


def weight_grads(both, result):
    modes = both.shape[2] // 2
    outer, inner = repeat_tables()
    outer = outer.astype(BF16)
    inner = inner.astype(BF16)
    scale = mode_scale(modes, modes // MY)
    real_sum = jnp.zeros((modes, C * C), F32)
    imag_sum = jnp.zeros((modes, C * C), F32)
    for sample in range(both.shape[0]):
        values = both[sample]
        field = dot(values[:C], outer, ((0,), (0,)))
        grads = dot(values[C:], inner, ((0,), (0,)))
        real_u, imag_u = field[:modes], field[modes:]
        real_d, imag_d = grads[:modes] * scale, grads[modes:] * scale
        real_sum = real_sum + (real_u * real_d + imag_u * imag_d)
        imag_sum = imag_sum + (real_u * imag_d - imag_u * real_d)
    for part, total in enumerate((real_sum, imag_sum)):
        result[part, 0] = total.reshape(result.shape[2:])


def pair_spectra(own, other, both):
    both[0] = own[...]
    both[1] = other[...]


def inverse_x(arrived, x_rows, result):
    blocks = x_blocks(x_rows)
    values = arrived[...].reshape(MX * C, arrived.shape[2])
    half = values.shape[1] // 2
    swapped = jnp.concatenate([-values[:, half:], values[:, :half]], axis=1)
    sums = dot(values, blocks[0], ((0,), (0,))) + dot(swapped, blocks[1], ((0,), (0,)))
    result[...] = jnp.broadcast_to(sums.astype(BF16)[None], result.shape)


def mixing_table(point, rows):
    local_x = rows // C
    row = lax.broadcasted_iota(jnp.int32, (rows, C), 0) // local_x
    pick = (row == lax.broadcasted_iota(jnp.int32, (rows, C), 1)).astype(BF16)
    spread = dot(pick, point[...], ((1,), (0,))).astype(BF16)
    spread = dot(spread, pick, ((1,), (1,)))
    left = lax.broadcasted_iota(jnp.int32, (rows, rows), 0) % local_x
    right = lax.broadcasted_iota(jnp.int32, (rows, rows), 1) % local_x
    return jnp.where(left == right, spread, 0.0).astype(BF16)


def inverse_y(own, y_tables, both, own_lines, grad_spec, spec_staged, spec_sem):
    weight_grads(both, spec_staged)
    spec_copy = pltpu.make_async_copy(spec_staged, grad_spec, spec_sem)
    spec_copy.start()
    y_table = y_tables[lax.axis_index("gy")]
    for index in range(own.shape[0]):
        block = dot(y_table, own[index], ((0,), (0,)))
        own_lines[index] = block.reshape(own_lines.shape[1:])
    spec_copy.wait()


def inverse_yz(
    own_lines, taken, grad_pre, z_table, y_tables, point, result, lines, staged, sems
):
    y_table = y_tables[lax.axis_index("gy")]
    rows = staged.shape[0]
    mixing = mixing_table(point, rows)
    side = lax.axis_index("gy") % 2
    per = own_lines.shape[1]
    for index in range(taken.shape[0]):
        block = dot(y_table, taken[index], ((0,), (0,)))
        lines[pl.ds((2 * index + 1 - side) * per, per)] = block.reshape(per, -1, rows)
        lines[pl.ds((2 * index + side) * per, per)] = own_lines[index]
    width = z_table.shape[1]
    copies = []
    for group in range(result.shape[1] // width):
        block = lines[:, group * GROUP : (group + 1) * GROUP, :]
        block = block.reshape(2 * MZ * GROUP, rows).astype(BF16)
        part = slice(group * width, (group + 1) * width)
        spectral = dot(block, z_table[...], ((0,), (0,)))
        mixed = dot(mixing, grad_pre[:, part], ((1,), (0,)))
        staged[:, part] = (spectral + mixed).astype(BF16)
        copy = pltpu.make_async_copy(
            staged.at[:, pl.ds(group * width, width)],
            result.at[:, pl.ds(group * width, width)],
            sems.at[group],
        )
        copy.start()
        copies.append(copy)
    for copy in copies:
        copy.wait()


VMEM = pl.BlockSpec(memory_space=pltpu.VMEM)
HBM = pl.BlockSpec(memory_space=pltpu.HBM)


def call(body, ins, outs, scratch=(), vmem=24):
    values = [
        pltpu.with_memory_space_constraint(value, spec.memory_space) for value, spec in ins
    ]
    specs = [spec for _, spec in ins]
    shapes = [
        pltpu.VMEM(shape, dtype) if spec is VMEM else jax.ShapeDtypeStruct(shape, dtype)
        for shape, dtype, spec in outs
    ]
    return pl.pallas_call(
        body,
        in_specs=specs,
        out_specs=[spec for _, _, spec in outs],
        out_shape=shapes,
        scratch_shapes=list(scratch),
        compiler_params=pltpu.CompilerParams(vmem_limit_bytes=vmem << 20),
    )(*values)


def run_forward_zy(fields, pre_act, cotangent, z_table, y_table, local_mz):
    rows, local_yz = fields.shape
    local_y = local_yz // NZ
    modes = MY * local_mz
    half = (MZ // local_mz // 2, 2 * modes, 2 * rows)
    whole = (rows, local_yz)
    dma = pltpu.SemaphoreType.DMA
    return call(
        forward_zy,
        [(fields, HBM), (pre_act, HBM), (cotangent, HBM), (z_table, HBM), (y_table, HBM)],
        [(whole, BF16, VMEM), (half, BF16, VMEM), (half, BF16, VMEM)],
        [pltpu.VMEM(whole, BF16)] * 3
        + [
            pltpu.VMEM(z_table.shape, BF16),
            pltpu.VMEM(y_table.shape[1:], BF16),
            pltpu.VMEM((2 * MZ, local_y, 2 * rows), BF16),
            dma((3, 2)),
            dma((2,)),
        ],
    )


def run_inverse_y(own, y_table, both, spec_shape):
    count, _, rows = own.shape
    return call(
        inverse_y,
        [(own, VMEM), (y_table, VMEM), (both, VMEM)],
        [
            ((count, MZ // count, y_table.shape[2] * count // MZ, rows), F32, VMEM),
            (spec_shape, F32, HBM),
        ],
        [pltpu.VMEM(spec_shape, F32), pltpu.SemaphoreType.DMA(())],
    )


def run_inverse_yz(own_lines, taken, grad_pre, z_table, y_table, point):
    rows, local_yz = grad_pre.shape
    local_y = local_yz // NZ
    groups = local_y // GROUP
    (grad_fields,) = call(
        inverse_yz,
        [
            (own_lines, VMEM),
            (taken, VMEM),
            (grad_pre, VMEM),
            (z_table, VMEM),
            (y_table, VMEM),
            (point, VMEM),
        ],
        [((rows, local_yz), BF16, HBM)],
        [
            pltpu.VMEM((2 * MZ, local_y, rows), F32),
            pltpu.VMEM((rows, local_yz), BF16),
            pltpu.SemaphoreType.DMA((groups,)),
        ],
    )
    return grad_fields


def exchange(pieces, axis, groups=None):
    return lax.all_to_all(
        pieces, axis, split_axis=0, concat_axis=0, tiled=True, axis_index_groups=groups
    )


def on_device(fields, pre_act, cotangent, spec_weight, point_weight):
    count_x = lax.axis_size("gx")
    count_y = lax.axis_size("gy")
    _, channels, local_x, local_yz = fields.shape
    local_y = local_yz // NZ
    local_mz = spec_weight.shape[3]
    rows = channels * local_x
    modes = MY * local_mz
    z_table = jnp.asarray(z_block_table())
    y_table = jnp.asarray(y_block_tables(count_y, local_y, local_mz))
    x_rows = jnp.asarray(x_row_tables(count_x, local_x))
    whole = (rows, local_yz)

    grad_pre, kept, given = run_forward_zy(
        fields.reshape(whole),
        pre_act.reshape(whole),
        cotangent.reshape(whole),
        z_table,
        y_table,
        local_mz,
    )
    other_side = [(i, i ^ 1) for i in range(count_y)]
    taken = lax.ppermute(given, "gy", other_side)
    (sums,) = call(add_halves, [(kept, VMEM), (taken, VMEM)], [(kept.shape, BF16, VMEM)])
    sides = [list(range(side, count_y, 2)) for side in range(2)]
    arrived = exchange(sums, "gy", sides)
    (pieces,) = call(
        forward_x,
        [(arrived, VMEM), (x_rows, VMEM)],
        [((count_x, 2 * C, 2 * modes), BF16, VMEM)],
    )
    arrived = exchange(pieces, "gx")
    spectrum, pieces = call(
        mode_products,
        [(arrived, VMEM), (spec_weight, VMEM)],
        [((2 * C, 2 * modes), BF16, VMEM), ((count_x, C, 2 * modes), BF16, VMEM)],
    )
    arrived = exchange(pieces, "gx")
    other = lax.ppermute(spectrum, "dp", [(0, 1), (1, 0)])
    (both,) = call(
        pair_spectra,
        [(spectrum, VMEM), (other, VMEM)],
        [((2,) + spectrum.shape, BF16, VMEM)],
    )
    (pieces,) = call(
        inverse_x,
        [(arrived, VMEM), (x_rows, VMEM)],
        [((count_y // 2, 2 * modes, rows), BF16, VMEM)],
    )
    own = exchange(pieces, "gy", sides)
    taken = lax.ppermute(own, "gy", other_side)
    own_lines, grad_spec = run_inverse_y(own, y_table, both, spec_weight.shape)
    grad_fields = run_inverse_yz(own_lines, taken, grad_pre, z_table, y_table, point_weight)
    return grad_fields.reshape(fields.shape), grad_spec


def solution(mesh):
    placed = (
        P("dp", None, "gx", "gy"),
        P("dp", None, "gx", "gy"),
        P("dp", None, "gx", "gy"),
        P(None, "gx", None, "gy", None),
        P(),
    )

    return jax.shard_map(
        on_device,
        mesh=mesh,
        in_specs=placed,
        out_specs=(P("dp", None, "gx", "gy"), P(None, "gx", None, "gy", None)),
        check_vma=False,
    )
```

```python
import math

import jax
import jax.numpy as jnp
import numpy as np
from jax import lax
from jax.experimental import pallas as pl
from jax.experimental.pallas import tpu as pltpu
from jax.sharding import PartitionSpec as P

C = 16
NX = 256
NY = 512
NZ = 64
MX = 32
MY = 32
MZ = 16
GROUP = 8

F32 = jnp.float32
BF16 = jnp.bfloat16


def signed_freqs(kept, length):
    index = np.arange(kept)
    return np.where(index < kept // 2, index, length - kept + index)


def cos_sin(freqs, points, length):
    turns = points[:, None] * freqs[None, :] % length
    angle = turns.astype(np.float32) * np.float32(2.0 * math.pi / length)
    return np.cos(angle).astype(np.float32), np.sin(angle).astype(np.float32)


def z_block_table():
    cosine, sine = cos_sin(np.arange(MZ), np.arange(NZ), NZ)
    parts = np.stack([cosine.T, -sine.T], axis=1)
    same = np.eye(GROUP, dtype=np.float32)
    table = parts[:, :, None, None, :] * same[None, None, :, :, None]
    return table.reshape(2 * MZ * GROUP, GROUP * NZ).astype(BF16)


def y_block_tables(count, local_y, local_mz):
    cosine, sine = cos_sin(signed_freqs(MY, NY), np.arange(NY), NY)
    upper = np.stack([cosine, sine], axis=-1)
    lower = np.stack([-sine, cosine], axis=-1)
    table = np.stack([upper, lower], axis=0)
    table = table.reshape(2, count, local_y, MY, 2).transpose(1, 0, 3, 4, 2)
    same = np.eye(local_mz, dtype=np.float32)
    table = table[:, :, :, None, None, :, :] * same[None, None, None, :, :, None, None]
    return table.reshape(count, 2 * MY * local_mz, local_mz * 2 * local_y).astype(BF16)


def x_row_tables(count, local_x):
    cosine, sine = cos_sin(signed_freqs(MX, NX), np.arange(NX), NX)
    table = np.stack([cosine, sine], axis=0).reshape(2, count, local_x, MX)
    table = table.transpose(1, 0, 3, 2)
    return np.tile(table, (1, 1, 1, 128 // local_x)).astype(BF16)


def dot(left, right, dims):
    return lax.dot_general(left, right, (dims, ((), ())), preferred_element_type=F32)


def gelu_slope(value):
    cdf = 0.5 * (1.0 + lax.erf(value * (1.0 / math.sqrt(2.0))))
    return cdf + value * jnp.exp(-0.5 * value * value) * (1.0 / math.sqrt(2.0 * math.pi))


def copies_in(sources, targets, sems):
    width = targets[0].shape[1] // sems.shape[1]
    copies = []
    for chunk in range(sems.shape[1]):
        lanes = pl.ds(chunk * width, width)
        copies.append(
            [
                pltpu.make_async_copy(
                    source.at[:, lanes], target.at[:, lanes], sems.at[index, chunk]
                )
                for index, (source, target) in enumerate(zip(sources, targets))
            ]
        )
    return copies


def forward_zy(
    fields, pre_act, cotangent, z_source, y_source, grad_pre, kept, given,
    fields_in, pre_in, cotangent_in, z_table, y_table, lines, sems, table_sems,
):
    groups = pre_act.shape[1] // z_source.shape[1]
    per_chunk = groups // sems.shape[1]
    tables = [
        pltpu.make_async_copy(z_source, z_table, table_sems.at[0]),
        pltpu.make_async_copy(y_source.at[lax.axis_index("gy")], y_table, table_sems.at[1]),
    ]
    copies = copies_in(
        (pre_act, cotangent, fields), (pre_in, cotangent_in, fields_in), sems
    )
    for copy in copies[0] + tables[:1]:
        copy.start()
    for chunk in copies[1:]:
        for copy in chunk:
            copy.start()
    tables[1].start()
    width = pre_in.shape[1] // groups
    pair = []
    for group in range(groups):
        if group % per_chunk == 0:
            for copy in copies[group // per_chunk]:
                copy.wait()
        part = slice(group * width, (group + 1) * width)
        slope = gelu_slope(pre_in[:, part].astype(F32))
        grad = (cotangent_in[:, part].astype(F32) * slope).astype(BF16)
        grad_pre[:, part] = grad
        both = jnp.concatenate([fields_in[:, part], grad], axis=0)
        if group == 0:
            tables[0].wait()
        spectra = dot(z_table[...], both, ((1,), (1,)))
        pair.append(spectra.reshape(2 * MZ, GROUP, both.shape[0]))
        if len(pair) == 2:
            rows = slice((group - 1) * GROUP, (group + 1) * GROUP)
            lines[:, rows, :] = jnp.concatenate(pair, axis=1).astype(BF16)
            pair = []
    tables[1].wait()
    side = lax.axis_index("gy") % 2
    count = 2 * kept.shape[0]
    per = 2 * MZ // count
    for index in range(count // 2):
        for pieces, offset in ((given, 1 - side), (kept, side)):
            first = (2 * index + offset) * per
            block = lines[pl.ds(first, per)]
            block = block.reshape(per * block.shape[1], block.shape[2])
            pieces[index] = dot(y_table[...], block, ((1,), (0,))).astype(BF16)


def add_halves(kept, taken, sums):
    sums[...] = (kept[...].astype(F32) + taken[...].astype(F32)).astype(BF16)


def add_up(arrived):
    total = arrived[0].astype(F32)
    for index in range(1, arrived.shape[0]):
        total = total + arrived[index].astype(F32)
    return total


def x_blocks(x_rows):
    lanes = x_rows.shape[3]
    owner = lax.broadcasted_iota(jnp.int32, (C, lanes), 1) // (lanes // C)
    mask = owner == lax.broadcasted_iota(jnp.int32, (C, lanes), 0)
    rows = x_rows[lax.axis_index("gx")].astype(F32)
    blocks = []
    for part in range(2):
        table = jnp.where(mask[None], rows[part][:, None, :], 0.0)
        blocks.append(table.reshape(MX * C, lanes).astype(BF16))
    return blocks


def forward_x(arrived, x_rows, pieces):
    blocks = x_blocks(x_rows)
    total = add_up(arrived)
    half = total.shape[0] // 2
    swapped = jnp.concatenate([total[half:], -total[:half]], axis=0).astype(BF16)
    total = total.astype(BF16)
    lanes = blocks[0].shape[1]
    for part in range(2):
        own = slice(part * lanes, (part + 1) * lanes)
        spectra = dot(blocks[0], total[:, own], ((1,), (1,)))
        spectra = spectra + dot(blocks[1], swapped[:, own], ((1,), (1,)))
        spectra = spectra.reshape(MX, C, spectra.shape[1]).astype(BF16)
        pieces[:, part * C : (part + 1) * C, :] = spectra


def mode_scale(rows, local_mz):
    line = lax.broadcasted_iota(jnp.int32, (rows, 1), 0) % local_mz
    line = line + lax.axis_index("gy") * local_mz
    return jnp.where(line == 0, 1.0, 2.0).astype(F32) / float(NX * NY * NZ)


def repeat_tables():
    lane = lax.broadcasted_iota(jnp.int32, (C, C * C), 1)
    row = lax.broadcasted_iota(jnp.int32, (C, C * C), 0)
    outer = (lane // C == row).astype(F32)
    inner = (lane % C == row).astype(F32)
    return outer, inner


def mode_products(arrived, weights, spectrum, grad_hat):
    total = add_up(arrived).astype(BF16)
    spectrum[...] = total
    modes = total.shape[1] // 2
    outer, inner = repeat_tables()
    grads = dot(total[C:], inner.astype(BF16), ((0,), (0,)))
    scale = mode_scale(modes, modes // MY)
    real_d = grads[:modes] * scale
    imag_d = grads[modes:] * scale
    real_w = weights[0, 0].astype(F32).reshape(modes, C * C)
    imag_w = weights[1, 0].astype(F32).reshape(modes, C * C)
    products = jnp.concatenate(
        [real_w * real_d + imag_w * imag_d, real_w * imag_d - imag_w * real_d], axis=0
    )
    values = None
    for _ in range(3):
        piece = products.astype(BF16)
        products = products - piece.astype(F32)
        term = dot(outer.astype(BF16), piece, ((1,), (1,)))
        values = term if values is None else values + term
    values = values.astype(BF16)
    grad_hat[...] = jnp.broadcast_to(values[None], grad_hat.shape)


def weight_grads(both, result):
    modes = both.shape[2] // 2
    outer, inner = repeat_tables()
    outer = outer.astype(BF16)
    inner = inner.astype(BF16)
    scale = mode_scale(modes, modes // MY)
    real_sum = jnp.zeros((modes, C * C), F32)
    imag_sum = jnp.zeros((modes, C * C), F32)
    for sample in range(both.shape[0]):
        values = both[sample]
        field = dot(values[:C], outer, ((0,), (0,)))
        grads = dot(values[C:], inner, ((0,), (0,)))
        real_u, imag_u = field[:modes], field[modes:]
        real_d, imag_d = grads[:modes] * scale, grads[modes:] * scale
        real_sum = real_sum + (real_u * real_d + imag_u * imag_d)
        imag_sum = imag_sum + (real_u * imag_d - imag_u * real_d)
    for part, total in enumerate((real_sum, imag_sum)):
        result[part, 0] = total.reshape(result.shape[2:])


def pair_spectra(own, other, both):
    both[0] = own[...]
    both[1] = other[...]


def inverse_x(arrived, x_rows, result):
    blocks = x_blocks(x_rows)
    values = arrived[...].reshape(MX * C, arrived.shape[2])
    half = values.shape[1] // 2
    swapped = jnp.concatenate([-values[:, half:], values[:, :half]], axis=1)
    sums = dot(values, blocks[0], ((0,), (0,))) + dot(swapped, blocks[1], ((0,), (0,)))
    result[...] = jnp.broadcast_to(sums.astype(BF16)[None], result.shape)


def mixing_table(point, rows):
    local_x = rows // C
    row = lax.broadcasted_iota(jnp.int32, (rows, C), 0) // local_x
    pick = (row == lax.broadcasted_iota(jnp.int32, (rows, C), 1)).astype(BF16)
    spread = dot(pick, point[...], ((1,), (0,))).astype(BF16)
    spread = dot(spread, pick, ((1,), (1,)))
    left = lax.broadcasted_iota(jnp.int32, (rows, rows), 0) % local_x
    right = lax.broadcasted_iota(jnp.int32, (rows, rows), 1) % local_x
    return jnp.where(left == right, spread, 0.0).astype(BF16)


def inverse_yz(
    arrived, grad_pre, z_table, y_tables, point, both, result, grad_spec,
    lines, staged, spec_staged, sems, spec_sem,
):
    y_table = y_tables[lax.axis_index("gy")]
    rows = staged.shape[0]
    mixing = mixing_table(point, rows)
    count = arrived.shape[0]
    per = 2 * MZ // count
    for index in range(count):
        block = dot(y_table, arrived[index], ((0,), (0,)))
        lines[index * per : (index + 1) * per] = block.reshape(per, -1, rows)
    weight_grads(both, spec_staged)
    spec_copy = pltpu.make_async_copy(spec_staged, grad_spec, spec_sem)
    spec_copy.start()
    width = z_table.shape[1]
    copies = [spec_copy]
    for group in range(result.shape[1] // width):
        block = lines[:, group * GROUP : (group + 1) * GROUP, :]
        block = block.reshape(2 * MZ * GROUP, rows).astype(BF16)
        part = slice(group * width, (group + 1) * width)
        spectral = dot(block, z_table[...], ((0,), (0,)))
        mixed = dot(mixing, grad_pre[:, part], ((1,), (0,)))
        staged[:, part] = (spectral + mixed).astype(BF16)
        copy = pltpu.make_async_copy(
            staged.at[:, pl.ds(group * width, width)],
            result.at[:, pl.ds(group * width, width)],
            sems.at[group],
        )
        copy.start()
        copies.append(copy)
    for copy in copies:
        copy.wait()


VMEM = pl.BlockSpec(memory_space=pltpu.VMEM)
HBM = pl.BlockSpec(memory_space=pltpu.HBM)


def call(body, ins, outs, scratch=(), vmem=24):
    values = [
        pltpu.with_memory_space_constraint(value, spec.memory_space) for value, spec in ins
    ]
    specs = [spec for _, spec in ins]
    shapes = [
        pltpu.VMEM(shape, dtype) if spec is VMEM else jax.ShapeDtypeStruct(shape, dtype)
        for shape, dtype, spec in outs
    ]
    return pl.pallas_call(
        body,
        in_specs=specs,
        out_specs=[spec for _, _, spec in outs],
        out_shape=shapes,
        scratch_shapes=list(scratch),
        compiler_params=pltpu.CompilerParams(vmem_limit_bytes=vmem << 20),
    )(*values)


def run_forward_zy(fields, pre_act, cotangent, z_table, y_table, local_mz):
    rows, local_yz = fields.shape
    local_y = local_yz // NZ
    modes = MY * local_mz
    half = (MZ // local_mz // 2, 2 * modes, 2 * rows)
    whole = (rows, local_yz)
    dma = pltpu.SemaphoreType.DMA
    return call(
        forward_zy,
        [(fields, HBM), (pre_act, HBM), (cotangent, HBM), (z_table, HBM), (y_table, HBM)],
        [(whole, BF16, VMEM), (half, BF16, VMEM), (half, BF16, VMEM)],
        [pltpu.VMEM(whole, BF16)] * 3
        + [
            pltpu.VMEM(z_table.shape, BF16),
            pltpu.VMEM(y_table.shape[1:], BF16),
            pltpu.VMEM((2 * MZ, local_y, 2 * rows), BF16),
            dma((3, 2)),
            dma((2,)),
        ],
    )


def run_inverse_yz(arrived, grad_pre, z_table, y_table, point, both, spec_shape):
    rows, local_yz = grad_pre.shape
    local_y = local_yz // NZ
    groups = local_y // GROUP
    return call(
        inverse_yz,
        [
            (arrived, VMEM),
            (grad_pre, VMEM),
            (z_table, VMEM),
            (y_table, VMEM),
            (point, VMEM),
            (both, VMEM),
        ],
        [((rows, local_yz), BF16, HBM), (spec_shape, F32, HBM)],
        [
            pltpu.VMEM((2 * MZ, local_y, rows), F32),
            pltpu.VMEM((rows, local_yz), BF16),
            pltpu.VMEM(spec_shape, F32),
            pltpu.SemaphoreType.DMA((groups,)),
            pltpu.SemaphoreType.DMA(()),
        ],
    )


def exchange(pieces, axis, groups=None):
    return lax.all_to_all(
        pieces, axis, split_axis=0, concat_axis=0, tiled=True, axis_index_groups=groups
    )


def on_device(fields, pre_act, cotangent, spec_weight, point_weight):
    count_x = lax.axis_size("gx")
    count_y = lax.axis_size("gy")
    _, channels, local_x, local_yz = fields.shape
    local_y = local_yz // NZ
    local_mz = spec_weight.shape[3]
    rows = channels * local_x
    modes = MY * local_mz
    z_table = jnp.asarray(z_block_table())
    y_table = jnp.asarray(y_block_tables(count_y, local_y, local_mz))
    x_rows = jnp.asarray(x_row_tables(count_x, local_x))
    whole = (rows, local_yz)

    grad_pre, kept, given = run_forward_zy(
        fields.reshape(whole),
        pre_act.reshape(whole),
        cotangent.reshape(whole),
        z_table,
        y_table,
        local_mz,
    )
    taken = lax.ppermute(given, "gy", [(i, i ^ 1) for i in range(count_y)])
    (sums,) = call(add_halves, [(kept, VMEM), (taken, VMEM)], [(kept.shape, BF16, VMEM)])
    sides = [list(range(side, count_y, 2)) for side in range(2)]
    arrived = exchange(sums, "gy", sides)
    (pieces,) = call(
        forward_x,
        [(arrived, VMEM), (x_rows, VMEM)],
        [((count_x, 2 * C, 2 * modes), BF16, VMEM)],
    )
    arrived = exchange(pieces, "gx")
    spectrum, pieces = call(
        mode_products,
        [(arrived, VMEM), (spec_weight, VMEM)],
        [((2 * C, 2 * modes), BF16, VMEM), ((count_x, C, 2 * modes), BF16, VMEM)],
    )
    arrived = exchange(pieces, "gx")
    other = lax.ppermute(spectrum, "dp", [(0, 1), (1, 0)])
    (both,) = call(
        pair_spectra,
        [(spectrum, VMEM), (other, VMEM)],
        [((2,) + spectrum.shape, BF16, VMEM)],
    )
    (pieces,) = call(
        inverse_x,
        [(arrived, VMEM), (x_rows, VMEM)],
        [((count_y, 2 * modes, rows), BF16, VMEM)],
    )
    arrived = exchange(pieces, "gy")
    grad_fields, grad_spec = run_inverse_yz(
        arrived, grad_pre, z_table, y_table, point_weight, both, spec_weight.shape
    )
    return grad_fields.reshape(fields.shape), grad_spec


def solution(mesh):
    placed = (
        P("dp", None, "gx", "gy"),
        P("dp", None, "gx", "gy"),
        P("dp", None, "gx", "gy"),
        P(None, "gx", None, "gy", None),
        P(),
    )

    return jax.shard_map(
        on_device,
        mesh=mesh,
        in_specs=placed,
        out_specs=(P("dp", None, "gx", "gy"), P(None, "gx", None, "gy", None)),
        check_vma=False,
    )
```
